32 devices in a mesh: layer: 4 (over z), row: 4 (over x, core), col: 2 (over y).
Axes of the slice: x: 2, y: 2, z: 4, core: 2. Of those that a mesh axis runs over, the one named last changes fastest.
Arguments:
- rhs_low: bfloat16 [4, 2, 2, 384, 512], P('layer', None, 'col'), may hold values from -6 to 6
- inv_low: bfloat16 [4, 2, 2, 384, 384], P('layer', None, 'col'), as said below
- blocks: bfloat16 [4, 4, 2, 2, 4, 384, 384], P('layer', 'row', 'col'), may hold values from -0.02734375 to 0.02734375
- targets: int32 [4, 4, 2, 2, 4], P('layer', 'row', 'col'), may hold values from 1 to 5, as said below
- rhs_anc: bfloat16 [16, 384, 512], P('row', None, ('layer', 'col')), may hold values from -6 to 6
- inv_anc: bfloat16 [16, 384, 384], P('row'), as said below
Outputs:
- solution_low: bfloat16 [4, 2, 2, 384, 512], P('layer', None, 'col', None, 'row')
- solution_anc: float32 [16, 384, 512], P('row', None, ('layer', 'col'))
The draws below stay inside these ranges and needn't reach their ends.
Inputs may be any that keep to these rules, and one draw needn't show every extreme that they name: For each g, r, c, l the 4 values targets[g, r, c, l, :] are distinct. A value t < 2 is greater than l; a value t >= 2 names ancestor r * 4 + t - 2. `inv_low`: each block is lower triangular. `inv_anc`: each block is lower triangular.
All inputs are finite; a program needn't handle non-finite values.
Results may differ from the reference program's by a relative error of at most 0.011.
Values may be sent and summed in bfloat16 or wider, within the bound.
A program may use at most 64 MiB of HBM per device.

```python
import jax
import jax.numpy as jnp
from jax import lax

W = 384
R = 512
LEVELS = 2
BPR = 4
LAYERS = 4
GRID_ROWS = 4
GRID_COLS = 2
ANC_ROW = 4
ANC = 16


def lower_block(key, count):
    first, second = jax.random.split(key)
    below = jax.random.normal(second, (count, W, W), jnp.float32) * 0.8 / jnp.sqrt(1.0 * W)
    middle = jax.random.uniform(first, (count, W), jnp.float32, 0.6, 1.4)
    return jnp.tril(below, -1) + middle[:, :, None] * jnp.eye(W, dtype=jnp.float32)[None]


def draw_inv_low(key, part):
    matrix = lower_block(jax.random.fold_in(key, 5), LAYERS * LEVELS * GRID_COLS)
    return matrix.reshape(LAYERS, LEVELS, GRID_COLS, W, W).astype(jnp.bfloat16)


def draw_inv_anc(key, part):
    matrix = lower_block(jax.random.fold_in(key, 11), ANC)
    return matrix.astype(jnp.bfloat16)


def draw_targets(key, part):
    key = jax.random.fold_in(key, 3)
    total_options = LEVELS + ANC_ROW
    full_shape = (LAYERS, GRID_ROWS, GRID_COLS, LEVELS, total_options)
    option = jnp.arange(total_options, dtype=jnp.int32).reshape(1, 1, 1, 1, -1)
    source = jnp.arange(LEVELS, dtype=jnp.int32).reshape(1, 1, 1, -1, 1)
    holder = jnp.arange(GRID_ROWS, dtype=jnp.int32).reshape(1, -1, 1, 1, 1)
    inside = (option > source) & (option < LEVELS) & (jnp.mod(holder - option, GRID_ROWS) < GRID_COLS)
    allowed = inside | (option >= LEVELS)
    scores = jax.random.randint(key, full_shape, 0, 1 << 20, dtype=jnp.int32) * total_options + option
    scores = jnp.where(allowed, scores, -1)
    picked = lax.top_k(scores, BPR)[1]
    return picked.astype(jnp.int32)


def steps_of(own_key, extent, cuts, smallest, largest):
    loudness, own = 1.0, jax.random.fold_in(own_key, 6)
    for position, shards_of in cuts:
        heights = jnp.exp(jax.random.uniform(jax.random.fold_in(own, position), (shards_of,), jnp.float32, smallest / len(cuts), largest / len(cuts)))
        loudness = loudness * jnp.repeat(heights, extent[position] // shards_of).reshape([-1 if axis == position else 1 for axis in range(len(extent))])
    return loudness


def centred(key, dims, spread, bound, cuts=(), held_as=jnp.bfloat16):
    array = jax.random.normal(key, dims, jnp.float32) * spread
    if len(cuts) > 0:
        array = steps_of(key, dims, cuts, -0.22, 0.18) * array
    return jnp.clip(array, min=-bound, max=bound).astype(held_as)


def setup_inputs(seed: int = 0) -> dict:
    keys = jax.random.split(jax.random.key(seed), 7)
    return {
        "rhs_low": centred(keys[0], (LAYERS, LEVELS, GRID_COLS, W, R), 1.0, 6.0, ((0, 4), (2, 2))),
        "inv_low": draw_inv_low(jax.random.fold_in(keys[6], 71), 0),
        "blocks": centred(keys[2], (LAYERS, GRID_ROWS, GRID_COLS, LEVELS, BPR, W, W), (128 * W) ** -0.5, 0.02734375, ((0, 4), (1, 4), (2, 2))),
        "targets": draw_targets(jax.random.fold_in(keys[6], 71), 0),
        "rhs_anc": centred(keys[4], (ANC, W, R), 1.0, 6.0, ((0, 4), (2, 8))),
        "inv_anc": draw_inv_anc(jax.random.fold_in(keys[6], 71), 0),
    }


def layer_solve(rhs_layer, inv_layer, block_layer, target_layer):
    collected = jnp.zeros((GRID_ROWS, LEVELS + ANC_ROW, W, R), jnp.float32)
    row_ids = jnp.broadcast_to(jnp.arange(GRID_ROWS, dtype=jnp.int32)[:, None, None], (GRID_ROWS, GRID_COLS, BPR))
    solved = []
    for current in range(LEVELS):
        owners = (current + jnp.arange(GRID_COLS, dtype=jnp.int32)) % GRID_ROWS
        partial_value = collected[owners, current]
        residual = (rhs_layer[current].astype(jnp.float32) - partial_value).astype(jnp.bfloat16)
        answer = jnp.einsum("cwv,cvk->cwk", inv_layer[current].astype(jnp.float32), residual.astype(jnp.float32)).astype(jnp.bfloat16)
        solved.append(answer)
        product = jnp.einsum("rcswv,cvk->rcswk", block_layer[:, :, current].astype(jnp.float32), answer.astype(jnp.float32))
        collected = collected.at[row_ids, target_layer[:, :, current]].add(product)
    return jnp.stack(solved, 0), collected[:, LEVELS:]


def reference(rhs_low, inv_low, blocks, targets, rhs_anc, inv_anc):
    def one_layer(members):
        return layer_solve(members[0], members[1], members[2], members[3])

    solution_low, ancestor_parts = lax.map(one_layer, (rhs_low, inv_low, blocks, targets))
    ancestor_partial = jnp.sum(ancestor_parts, axis=0).reshape(ANC, W, R)
    residual = (rhs_anc.astype(jnp.float32) - ancestor_partial).astype(jnp.bfloat16)
    solution_anc = jnp.einsum("awv,avk->awk", inv_anc.astype(jnp.float32), residual.astype(jnp.float32))
    return solution_low, solution_anc
```

```python
import contextlib
import functools

import jax
import jax.numpy as jnp
from jax import lax
from jax.experimental import pallas as pl
from jax.experimental.pallas import tpu as pltpu
from jax.sharding import PartitionSpec as P

MESH = pl.DeviceIdType.MESH
F32 = jnp.float32
BF16 = jnp.bfloat16


def scope(name):
    return contextlib.nullcontext()


def dot_t(left, right):
    return lax.dot_general(left, right, (((1,), (1,)), ((), ())), preferred_element_type=F32)


def flag(condition):
    return condition.astype(jnp.int32)


def ranked(layer, layers):
    keys = []
    for j in range(layers):
        keys.append(flag(layer == j) * 1000 * layers - 2 * layers * jnp.abs(layer - j) - j)
    order = [0] * layers
    for j in range(layers):
        rank = 0
        for other in range(layers):
            if other != j:
                rank = rank + flag(keys[other] < keys[j])
        order = [order[k] + j * flag(rank == k) for k in range(layers)]
    return order


def kernel(
    sizes,
    targets_hbm,
    rhs_hbm,
    inv_hbm,
    blocks_hbm,
    rhs_anc_hbm,
    inv_anc_hbm,
    low_out,
    anc_out,
    rhs,
    inv,
    blocks0,
    blocks1,
    rhs_anc,
    inv_anc,
    x0,
    x1,
    part,
    part_in,
    rhs_t,
    base,
    packed,
    y_in,
    z_out,
    z_in,
    targets,
    load_sem,
    p_send,
    p_recv,
    x_send,
    x_recv,
    y_send,
    y_recv,
    z_send,
    z_recv,
):
    layers, rows, cols = sizes
    layer, row, col = (lax.axis_index(a) for a in ("layer", "row", "col"))
    slots = blocks0.shape[0]
    anc_row, narrow, width = rhs_anc.shape
    share = x1.shape[1]
    halves = packed.shape[2]
    per_half = anc_row // halves
    chips = rows // 2
    last = layers - 1

    chip, core = row // 2, row % 2
    mate = row + 1 - 2 * core
    order = ranked(layer, layers)
    goal = (row + rows - 1) % rows
    active = goal < cols
    owner = (1 + col) % rows

    barrier = pltpu.get_barrier_semaphore()

    def greet(device):
        pl.semaphore_signal(barrier, inc=1, device_id=device, device_id_type=MESH)

    greet({"row": mate})
    for d in range(1, cols):
        greet({"col": (col + d) % cols})
    for step in (-1, 1):

        @pl.when(jnp.logical_and(layer + step >= 0, layer + step < layers))
        def _():
            greet({"layer": layer + step})

    for cc in range(cols):

        @pl.when(jnp.logical_or(row != owner, col != cc))
        def _():
            greet({"row": owner, "col": cc})

    @pl.when(active)
    def _():
        for r in range(rows):

            @pl.when(jnp.logical_or(row != r, col != goal))
            def _():
                greet({"row": r, "col": goal})

    met = 1 + (cols - 1) + flag(layer > 0) + flag(layer < last)
    met = met + cols - flag(row == owner)
    met = met + flag(active) * (rows - flag(col == goal))

    loads = [
        pltpu.make_async_copy(inv_hbm.at[0], inv.at[0], load_sem.at[0]),
        pltpu.make_async_copy(rhs_hbm.at[0], rhs.at[0], load_sem.at[1]),
        pltpu.make_async_copy(blocks_hbm.at[0], blocks0, load_sem.at[2]),
        pltpu.make_async_copy(inv_hbm.at[1], inv.at[1], load_sem.at[3]),
        pltpu.make_async_copy(rhs_hbm.at[1], rhs.at[1], load_sem.at[4]),
        pltpu.make_async_copy(blocks_hbm.at[1], blocks1, load_sem.at[5]),
        pltpu.make_async_copy(inv_anc_hbm, inv_anc, load_sem.at[6]),
        pltpu.make_async_copy(rhs_anc_hbm, rhs_anc, load_sem.at[7]),
        pltpu.make_async_copy(targets_hbm, targets, load_sem.at[8]),
    ]
    for load in loads:
        load.start()

    def listed(level, target):
        index, found = jnp.int32(0), jnp.int32(0)
        for s in range(slots):
            hit = (targets[level, s] == target).astype(jnp.int32)
            index = index + hit * s
            found = found + hit
        return (blocks0, blocks1)[level][index], found.astype(F32)

    def span(j):
        return pl.ds(pl.multiple_of(j * share, share), share)

    with scope("x0"):
        loads[0].wait()
        loads[1].wait()
        first = jnp.dot(inv[0], rhs[0], preferred_element_type=F32)
        x0[...] = first.T.astype(BF16)

    loads[8].wait()
    loads[2].wait()

    def p_copy(k, ch):
        return pltpu.make_async_remote_copy(
            src_ref=part.at[k],
            dst_ref=part_in.at[k // 2, col],
            send_sem=p_send.at[k, ch],
            recv_sem=p_recv.at[k // 2, col],
            device_id={"row": 2 * ch + k % 2, "col": goal},
            device_id_type=MESH,
        )

    def here(k, ch):
        return jnp.logical_and(goal == col, row == 2 * ch + k % 2)

    def part_of(k):
        block, found = listed(0, 1)
        part[k] = (dot_t(x0[span(order[k]), :], block) * found).astype(BF16)

    @pl.when(active)
    def _():
        part_of(0)

    with scope("barr"):
        pl.semaphore_wait(barrier, met)

    with scope("part"):

        @pl.when(active)
        def _():
            for k in range(rows):
                if k:
                    part_of(k)
                for ch in range(chips):

                    @pl.when(jnp.logical_not(here(k, ch)))
                    def _():
                        p_copy(k, ch).start()

                    @pl.when(here(k, ch))
                    def _():
                        part_in[k // 2, col] = part[k]

    loads[3].wait()
    loads[4].wait()
    rhs_t[...] = rhs[1].astype(F32).T

    with scope("base"):
        for a in range(anc_row):
            block, found = listed(0, a + 2)
            base[:, a * width : (a + 1) * width] = dot_t(x0[...], block) * found

    for j in range(rows):

        @pl.when(row == j)
        def _():
            low_out[0] = x0[j * share : (j + 1) * share, :].astype(F32).T.astype(BF16)

    @pl.when(layer == 0)
    def _():
        z_in[0] = jnp.zeros_like(z_in[0])

    @pl.when(layer == last)
    def _():
        z_in[layers] = jnp.zeros_like(z_in[layers])

    loads[5].wait()

    def own(m):
        return order[2 * m] + core * (order[2 * m + 1] - order[2 * m])

    def x_copy(m):
        return pltpu.make_async_remote_copy(
            src_ref=x1.at[own(m)],
            dst_ref=x1.at[own(m)],
            send_sem=x_send.at[m],
            recv_sem=x_recv.at[m],
            device_id={"row": mate},
            device_id_type=MESH,
        )

    def solve(m):
        for cc in range(cols):

            @pl.when(jnp.logical_or(col != cc, row != owner))
            def _():
                pltpu.make_async_remote_copy(
                    src_ref=part.at[0],
                    dst_ref=part_in.at[m, cc],
                    send_sem=p_send.at[0, 0],
                    recv_sem=p_recv.at[m, cc],
                    device_id={"row": mate},
                    device_id_type=MESH,
                ).wait_recv()

        total = part_in[m, 0].astype(F32)
        for cc in range(1, cols):
            total = total + part_in[m, cc].astype(F32)
        residual = (rhs_t[span(own(m)), :] - total).astype(BF16)
        x1[own(m)] = dot_t(residual, inv[1]).astype(BF16)
        x_copy(m).start()

    def y_copy(d, k, h):
        cc = (col + d) % cols
        return pltpu.make_async_remote_copy(
            src_ref=packed.at[cc, k, h],
            dst_ref=y_in.at[d - 1, k, h],
            send_sem=y_send.at[d - 1, k, h],
            recv_sem=y_recv.at[d - 1, k, h],
            device_id={"col": cc},
            device_id_type=MESH,
        )

    def products(k):
        @pl.when(core != k % 2)
        def _():
            x_copy(k // 2).wait_recv()

        j = order[k]
        for a in range(anc_row):
            block, found = listed(1, a + 2)
            at = slice(a * width, (a + 1) * width)
            value = base[span(j), at] + dot_t(x1[j], block) * found
            value = value.astype(BF16)
            within = a % per_half * width
            for cc in range(cols):
                packed[cc, k, a // per_half, :, within : within + width] = value[
                    cc * narrow : (cc + 1) * narrow
                ]
            if a % per_half == per_half - 1:
                for d in range(1, cols):
                    y_copy(d, k, a // per_half).start()

    def z_copy(k, h):
        j = order[k]
        toward = layer + 2 * flag(j > layer) - 1
        slot = j + flag(j == layer - 1) * (layers - j)
        return pltpu.make_async_remote_copy(
            src_ref=z_out.at[k, h],
            dst_ref=z_in.at[slot, h],
            send_sem=z_send.at[k, h],
            recv_sem=z_recv.at[slot, h],
            device_id={"layer": toward},
            device_id_type=MESH,
        )

    def z_wait(slot, h):
        pltpu.make_async_remote_copy(
            src_ref=z_out.at[0, h],
            dst_ref=z_in.at[slot, h],
            send_sem=z_send.at[0, h],
            recv_sem=z_recv.at[slot, h],
            device_id={"layer": (layer + 1) % layers},
            device_id_type=MESH,
        ).wait_recv()

    def merged(k, h):
        for d in range(1, cols):
            y_copy(d, k, h).wait_recv()
        value = packed[col, k, h].astype(F32)
        for d in range(1, cols):
            value = value + y_in[d - 1, k, h].astype(F32)
        return value

    def merge(k, h):
        with scope("y%d%d" % (k, h)):
            value = merged(k, h)
        j = order[k]
        passing = jnp.logical_or(
            jnp.logical_and(j > layer, layer > 0), jnp.logical_and(j < layer, layer < last)
        )

        with scope("z%d%d" % (k, h)):

            @pl.when(passing)
            def _():
                z_wait(j, h)
                z_out[k, h] = (value + z_in[j, h].astype(F32)).astype(BF16)

            @pl.when(jnp.logical_not(passing))
            def _():
                z_out[k, h] = value.astype(BF16)

        z_copy(k, h).start()

    for k in range(rows):
        if k % 2 == 0:
            with scope("x1_%d" % (k // 2)):
                solve(k // 2)
        with scope("p%d" % k):
            products(k)

    low_out[1] = x1[row].astype(F32).T.astype(BF16)
    for k in range(rows - 1):
        for h in range(halves):
            merge(k, h)

    loads[6].wait()
    loads[7].wait()
    with scope("zown"):

        @pl.when(layer > 0)
        def _():
            for h in range(halves):
                z_wait(layer, h)

        @pl.when(layer < last)
        def _():
            for h in range(halves):
                z_wait(layers, h)

    for h in range(halves):
        with scope("yown%d" % h):
            value = merged(rows - 1, h)
        with scope("fin%d" % h):
            value = value + z_in[layer, h].astype(F32) + z_in[layers, h].astype(F32)
            for within in range(per_half):
                a = h * per_half + within
                piece = value[:, within * width : (within + 1) * width]
                residual = (rhs_anc[a].astype(F32) - piece).astype(BF16)
                anc_out[a] = dot_t(residual, inv_anc[a])

    with scope("sent"):

        @pl.when(active)
        def _():
            for k in range(rows):
                for ch in range(chips):

                    @pl.when(jnp.logical_not(here(k, ch)))
                    def _():
                        p_copy(k, ch).wait_send()

        for m in range(chips):
            x_copy(m).wait_send()
        for k in range(rows):
            for h in range(halves):
                for d in range(1, cols):
                    y_copy(d, k, h).wait_send()
                if k < rows - 1:
                    z_copy(k, h).wait_send()


def hand_over(low, anc, low_out, anc_out, sem):
    first = pltpu.make_async_copy(anc, anc_out, sem.at[0])
    second = pltpu.make_async_copy(low, low_out, sem.at[1])
    first.start()
    second.start()
    first.wait()
    second.wait()


def on_device(sizes, rhs_low, inv_low, blocks, targets, rhs_anc, inv_anc):
    layers, rows, cols = sizes
    levels, slots = blocks.shape[3], blocks.shape[4]
    width, cases = rhs_low.shape[3], rhs_low.shape[4]
    anc_row, narrow = rhs_anc.shape[0], rhs_anc.shape[2]
    share = cases // rows
    halves = 2 if anc_row % 2 == 0 else 1
    chips = rows // 2
    assert levels == 2 and layers == rows and rows % 2 == 0 and cols <= rows
    assert cols * narrow == share
    any_space = pl.BlockSpec(memory_space=pltpu.HBM)
    dma = pltpu.SemaphoreType.DMA
    wide = anc_row * width // halves
    low, anc = pl.pallas_call(
        functools.partial(kernel, sizes),
        out_shape=(
            pltpu.VMEM((levels, width, share), BF16),
            pltpu.VMEM((anc_row, narrow, width), F32),
        ),
        in_specs=[any_space] * 6,
        out_specs=(pl.BlockSpec(memory_space=pltpu.VMEM), pl.BlockSpec(memory_space=pltpu.VMEM)),
        scratch_shapes=[
            pltpu.VMEM((levels, width, cases), BF16),
            pltpu.VMEM((levels, width, width), BF16),
            pltpu.VMEM((slots, width, width), BF16),
            pltpu.VMEM((slots, width, width), BF16),
            pltpu.VMEM((anc_row, narrow, width), BF16),
            pltpu.VMEM((anc_row, width, width), BF16),
            pltpu.VMEM((cases, width), BF16),
            pltpu.VMEM((rows, share, width), BF16),
            pltpu.VMEM((rows, share, width), BF16),
            pltpu.VMEM((chips, cols, share, width), BF16),
            pltpu.VMEM((cases, width), F32),
            pltpu.VMEM((cases, anc_row * width), F32),
            pltpu.VMEM((cols, rows, halves, narrow, wide), BF16),
            pltpu.VMEM((cols - 1, rows, halves, narrow, wide), BF16),
            pltpu.VMEM((rows - 1, halves, narrow, wide), BF16),
            pltpu.VMEM((layers + 1, halves, narrow, wide), BF16),
            pltpu.SMEM((levels, slots), jnp.int32),
            dma((9,)),
            dma((rows, chips)),
            dma((chips, cols)),
            dma((chips,)),
            dma((chips,)),
            dma((cols - 1, rows, halves)),
            dma((cols - 1, rows, halves)),
            dma((rows - 1, halves)),
            dma((layers + 1, halves)),
        ],
        compiler_params=pltpu.CompilerParams(
            collective_id=0, has_side_effects=True, vmem_limit_bytes=56 * 1024 * 1024
        ),
    )(
        targets.reshape(levels, slots),
        rhs_low.reshape(levels, width, cases),
        inv_low.reshape(levels, width, width),
        blocks.reshape(levels, slots, width, width),
        rhs_anc.transpose(0, 2, 1),
        inv_anc,
    )
    low, anc = pl.pallas_call(
        hand_over,
        out_shape=(
            jax.ShapeDtypeStruct(low.shape, low.dtype),
            jax.ShapeDtypeStruct(anc.shape, anc.dtype),
        ),
        in_specs=[pl.BlockSpec(memory_space=pltpu.VMEM)] * 2,
        out_specs=(any_space, any_space),
        scratch_shapes=[dma((2,))],
        compiler_params=pltpu.CompilerParams(vmem_limit_bytes=4 * 1024 * 1024),
    )(low, anc)
    return low[None, :, None], anc.transpose(0, 2, 1)


def solution(mesh):
    sizes = tuple(mesh.shape[a] for a in ("layer", "row", "col"))
    in_specs = (
        P("layer", None, "col", None, None),
        P("layer", None, "col", None, None),
        P("layer", "row", "col", None, None, None, None),
        P("layer", "row", "col", None, None),
        P("row", None, ("layer", "col")),
        P("row", None, None),
    )
    out_specs = (P("layer", None, "col", None, "row"), P("row", None, ("layer", "col")))
    return jax.shard_map(
        functools.partial(on_device, sizes),
        mesh=mesh,
        in_specs=in_specs,
        out_specs=out_specs,
        check_vma=False,
    )
```

```python
import contextlib
import functools

import jax
import jax.numpy as jnp
from jax import lax
from jax.experimental import pallas as pl
from jax.experimental.pallas import tpu as pltpu
from jax.sharding import PartitionSpec as P

MESH = pl.DeviceIdType.MESH
F32 = jnp.float32
BF16 = jnp.bfloat16


def scope(name):
    return contextlib.nullcontext()


def dot_t(left, right):
    return lax.dot_general(left, right, (((1,), (1,)), ((), ())), preferred_element_type=F32)


def flag(condition):
    return condition.astype(jnp.int32)


def ranked(layer, layers):
    low = flag(layer < layers // 2)
    far, near = low * (layers - 1), (1 - low) * (layers - 1)
    keys = []
    for j in range(layers):
        key = -2 * layers * jnp.abs(layer - j) - j
        key = key - 1000 * layers * flag(far == j) + 1000 * layers * flag(near == j)
        keys.append(key + 5000 * layers * flag(layer == j))
    order = [0] * layers
    for j in range(layers):
        rank = 0
        for other in range(layers):
            if other != j:
                rank = rank + flag(keys[other] < keys[j])
        order = [order[k] + j * flag(rank == k) for k in range(layers)]
    return order


def kernel(
    sizes,
    targets_hbm,
    rhs_hbm,
    inv_hbm,
    blocks_hbm,
    rhs_anc_hbm,
    inv_anc_hbm,
    low_out,
    anc_out,
    rhs,
    inv,
    blocks0,
    blocks1,
    rhs_anc,
    inv_anc,
    x0,
    x1,
    part,
    part_in,
    rhs_t,
    base,
    packed,
    y_in,
    z_out,
    z_in,
    r_in,
    targets,
    load_sem,
    p_send,
    p_recv,
    x_send,
    x_recv,
    y_send,
    y_recv,
    z_send,
    z_recv,
    r_send,
    r_recv,
):
    layers, rows, cols = sizes
    layer, row, col = (lax.axis_index(a) for a in ("layer", "row", "col"))
    slots = blocks0.shape[0]
    anc_row, narrow, width = rhs_anc.shape
    share = x1.shape[1]
    halves = packed.shape[2]
    per_half = anc_row // halves
    chips = rows // 2
    last = layers - 1

    chip, core = row // 2, row % 2
    mate = row + 1 - 2 * core
    order = ranked(layer, layers)
    goal = (row + rows - 1) % rows
    active = goal < cols
    owner = (1 + col) % rows

    barrier = pltpu.get_barrier_semaphore()

    def greet(device):
        pl.semaphore_signal(barrier, inc=1, device_id=device, device_id_type=MESH)

    greet({"row": mate})
    for d in range(1, cols):
        greet({"col": (col + d) % cols})
    for step in (-1, 1):

        @pl.when(jnp.logical_and(layer + step >= 0, layer + step < layers))
        def _():
            greet({"layer": layer + step})

    for cc in range(cols):

        @pl.when(jnp.logical_or(row != owner, col != cc))
        def _():
            greet({"row": owner, "col": cc})

    @pl.when(active)
    def _():
        for r in range(rows):

            @pl.when(jnp.logical_or(row != r, col != goal))
            def _():
                greet({"row": r, "col": goal})

    met = 1 + (cols - 1) + flag(layer > 0) + flag(layer < last)
    met = met + cols - flag(row == owner)
    met = met + flag(active) * (rows - flag(col == goal))

    loads = [
        pltpu.make_async_copy(inv_hbm.at[0], inv.at[0], load_sem.at[0]),
        pltpu.make_async_copy(rhs_hbm.at[0], rhs.at[0], load_sem.at[1]),
        pltpu.make_async_copy(blocks_hbm.at[0], blocks0, load_sem.at[2]),
        pltpu.make_async_copy(inv_hbm.at[1], inv.at[1], load_sem.at[3]),
        pltpu.make_async_copy(rhs_hbm.at[1], rhs.at[1], load_sem.at[4]),
        pltpu.make_async_copy(blocks_hbm.at[1], blocks1, load_sem.at[5]),
        pltpu.make_async_copy(inv_anc_hbm, inv_anc, load_sem.at[6]),
        pltpu.make_async_copy(rhs_anc_hbm, rhs_anc, load_sem.at[7]),
        pltpu.make_async_copy(targets_hbm, targets, load_sem.at[8]),
    ]
    for load in loads:
        load.start()

    def listed(level, target):
        index, found = jnp.int32(0), jnp.int32(0)
        for s in range(slots):
            hit = (targets[level, s] == target).astype(jnp.int32)
            index = index + hit * s
            found = found + hit
        return (blocks0, blocks1)[level][index], found.astype(F32)

    def span(j):
        return pl.ds(pl.multiple_of(j * share, share), share)

    with scope("x0"):
        loads[0].wait()
        loads[1].wait()
        first = jnp.dot(inv[0], rhs[0], preferred_element_type=F32)
        x0[...] = first.T.astype(BF16)

    loads[8].wait()
    loads[2].wait()

    def p_copy(k, ch):
        return pltpu.make_async_remote_copy(
            src_ref=part.at[k],
            dst_ref=part_in.at[k // 2, col],
            send_sem=p_send.at[k, ch],
            recv_sem=p_recv.at[k // 2, col],
            device_id={"row": 2 * ch + k % 2, "col": goal},
            device_id_type=MESH,
        )

    def here(k, ch):
        return jnp.logical_and(goal == col, row == 2 * ch + k % 2)

    def part_of(k):
        block, found = listed(0, 1)
        part[k] = (dot_t(x0[span(order[k]), :], block) * found).astype(BF16)

    @pl.when(active)
    def _():
        part_of(0)

    with scope("barr"):
        pl.semaphore_wait(barrier, met)

    with scope("part"):

        @pl.when(active)
        def _():
            for k in range(rows):
                if k:
                    part_of(k)
                for ch in range(chips):

                    @pl.when(jnp.logical_not(here(k, ch)))
                    def _():
                        p_copy(k, ch).start()

                    @pl.when(here(k, ch))
                    def _():
                        part_in[k // 2, col] = part[k]

    loads[3].wait()
    loads[4].wait()
    rhs_t[...] = rhs[1].astype(F32).T

    with scope("base"):
        for a in range(anc_row):
            block, found = listed(0, a + 2)
            base[:, a * width : (a + 1) * width] = dot_t(x0[...], block) * found

    for j in range(rows):

        @pl.when(row == j)
        def _():
            low_out[0] = x0[j * share : (j + 1) * share, :].astype(F32).T.astype(BF16)

    @pl.when(layer == 0)
    def _():
        z_in[0, 0] = jnp.zeros_like(z_in[0, 0])

    @pl.when(layer == last)
    def _():
        z_in[layers, 0] = jnp.zeros_like(z_in[layers, 0])

    loads[5].wait()

    def own(m):
        return order[2 * m] + core * (order[2 * m + 1] - order[2 * m])

    def x_copy(m):
        return pltpu.make_async_remote_copy(
            src_ref=x1.at[own(m)],
            dst_ref=x1.at[own(m)],
            send_sem=x_send.at[m],
            recv_sem=x_recv.at[m],
            device_id={"row": mate},
            device_id_type=MESH,
        )

    def solve(m):
        for cc in range(cols):

            @pl.when(jnp.logical_or(col != cc, row != owner))
            def _():
                pltpu.make_async_remote_copy(
                    src_ref=part.at[0],
                    dst_ref=part_in.at[m, cc],
                    send_sem=p_send.at[0, 0],
                    recv_sem=p_recv.at[m, cc],
                    device_id={"row": mate},
                    device_id_type=MESH,
                ).wait_recv()

        total = part_in[m, 0].astype(F32)
        for cc in range(1, cols):
            total = total + part_in[m, cc].astype(F32)
        residual = (rhs_t[span(own(m)), :] - total).astype(BF16)
        x1[own(m)] = dot_t(residual, inv[1]).astype(BF16)
        x_copy(m).start()

    def y_copy(d, k, h):
        cc = (col + d) % cols
        return pltpu.make_async_remote_copy(
            src_ref=packed.at[cc, k, h],
            dst_ref=y_in.at[d - 1, k, h],
            send_sem=y_send.at[d - 1, k, h],
            recv_sem=y_recv.at[d - 1, k, h],
            device_id={"col": cc},
            device_id_type=MESH,
        )

    def products(k):
        @pl.when(core != k % 2)
        def _():
            x_copy(k // 2).wait_recv()

        j = order[k]
        for a in range(anc_row):
            block, found = listed(1, a + 2)
            at = slice(a * width, (a + 1) * width)
            value = base[span(j), at] + dot_t(x1[j], block) * found
            value = value.astype(BF16)
            within = a % per_half * width
            for cc in range(cols):
                packed[cc, k, a // per_half, :, within : within + width] = value[
                    cc * narrow : (cc + 1) * narrow
                ]
            if a % per_half == per_half - 1:
                sent(k, a // per_half)

    end = jnp.logical_or(layer == 0, layer == last)
    middle = jnp.logical_or(layer == layers // 2 - 1, layer == layers // 2)
    onward = layer + 2 * flag(order[0] > layer) - 1

    def sent(k, h):
        if k == 0 and h == 0:

            @pl.when(end)
            def _():
                for d in range(1, cols + 1):
                    r_copy(d).start()

        elif k < rows - 2:
            exchange(k, h)
        elif k == rows - 2 and h == halves - 1:
            for other in reversed(range(1, halves)):
                exchange(k, other)

            @pl.when(jnp.logical_not(middle))
            def _():
                exchange(k, 0)

        elif k == rows - 1:

            @pl.when(jnp.logical_not(middle))
            def _():
                exchange(k, h)

    def exchange(k, h):
        for d in range(1, cols):
            y_copy(d, k, h).start()

    def r_copy(d):
        cc = (col + d) % cols
        return pltpu.make_async_remote_copy(
            src_ref=packed.at[cc, 0, 0],
            dst_ref=r_in.at[flag(middle), d - 1],
            send_sem=r_send.at[d - 1],
            recv_sem=r_recv.at[flag(middle), d - 1],
            device_id={"layer": onward},
            device_id_type=MESH,
        )

    def r_add(slot, k, d):
        pltpu.make_async_remote_copy(
            src_ref=packed.at[col, 0, 0],
            dst_ref=r_in.at[slot, d - 1],
            send_sem=r_send.at[d - 1],
            recv_sem=r_recv.at[slot, d - 1],
            device_id={"layer": onward},
            device_id_type=MESH,
        ).wait_recv()
        cc = (col + d) % cols
        value = packed[cc, k, 0].astype(F32) + r_in[slot, d - 1].astype(F32)
        packed[cc, k, 0] = value.astype(BF16)

    def z_copy(k, h):
        j = order[k]
        toward = layer + 2 * flag(j > layer) - 1
        slot = j + flag(j == layer - 1) * (layers - j)
        if k == 0:
            toward = toward + flag(middle) * (j - toward)
            slot = slot + flag(middle) * flag(j == last) * (layers - slot)
        return pltpu.make_async_remote_copy(
            src_ref=z_out.at[k, h],
            dst_ref=z_in.at[slot, h],
            send_sem=z_send.at[k, h],
            recv_sem=z_recv.at[slot, h],
            device_id={"layer": toward},
            device_id_type=MESH,
        )

    def z_wait(slot, h):
        pltpu.make_async_remote_copy(
            src_ref=z_out.at[0, h],
            dst_ref=z_in.at[slot, h],
            send_sem=z_send.at[0, h],
            recv_sem=z_recv.at[slot, h],
            device_id={"layer": (layer + 1) % layers},
            device_id_type=MESH,
        ).wait_recv()

    def merged(k, h):
        for d in range(1, cols):
            y_copy(d, k, h).wait_recv()
        value = packed[col, k, h].astype(F32)
        for d in range(1, cols):
            value = value + y_in[d - 1, k, h].astype(F32)
        return value

    def merge(k, h):
        with scope("y%d%d" % (k, h)):
            value = merged(k, h)
        j = order[k]
        passing = jnp.logical_or(
            jnp.logical_and(j > layer, layer > 0), jnp.logical_and(j < layer, layer < last)
        )
        if k == rows - 2:
            passing = jnp.logical_and(passing, jnp.logical_not(middle))

        with scope("z%d%d" % (k, h)):

            @pl.when(passing)
            def _():
                z_wait(j, h)
                z_out[k, h] = (value + z_in[j, h].astype(F32)).astype(BF16)

            @pl.when(jnp.logical_not(passing))
            def _():
                z_out[k, h] = value.astype(BF16)

        z_copy(k, h).start()

    for k in range(rows):
        if k % 2 == 0:
            with scope("x1_%d" % (k // 2)):
                solve(k // 2)
        with scope("p%d" % k):
            products(k)

    low_out[1] = x1[row].astype(F32).T.astype(BF16)

    with scope("rf"):

        @pl.when(jnp.logical_not(end))
        def _():
            for d in range(1, cols + 1):
                r_add(0, 0, d)
                r_copy(d).start()

    with scope("rn"):

        @pl.when(middle)
        def _():
            for d in range(1, cols):
                r_add(1, rows - 2, d)
            exchange(rows - 2, 0)
            for h in range(halves):
                exchange(rows - 1, h)

    for h in range(1, halves):
        merge(0, h)

    with scope("rw"):

        @pl.when(middle)
        def _():
            r_add(1, rows - 2, cols)

    before = [(k, h) for k in range(1, rows - 2) for h in range(halves)]
    after = [(rows - 2, h) for h in reversed(range(halves))]

    @pl.when(jnp.logical_not(middle))
    def _():
        for k, h in before + after:
            merge(k, h)

    @pl.when(middle)
    def _():
        for k, h in before[:-1] + after[:-1] + before[-1:] + after[-1:]:
            merge(k, h)

    loads[6].wait()
    loads[7].wait()
    with scope("zown"):

        for h in range(halves):
            for slot, edge in ((layer, layer == 0), (layers, layer == last)):
                if h:
                    z_wait(slot, h)
                else:

                    @pl.when(jnp.logical_not(edge))
                    def _():
                        z_wait(slot, h)

    for h in range(halves):
        with scope("yown%d" % h):
            value = merged(rows - 1, h)
        with scope("fin%d" % h):
            value = value + z_in[layer, h].astype(F32) + z_in[layers, h].astype(F32)
            for within in range(per_half):
                a = h * per_half + within
                piece = value[:, within * width : (within + 1) * width]
                residual = (rhs_anc[a].astype(F32) - piece).astype(BF16)
                anc_out[a] = dot_t(residual, inv_anc[a])

    with scope("sent"):

        @pl.when(active)
        def _():
            for k in range(rows):
                for ch in range(chips):

                    @pl.when(jnp.logical_not(here(k, ch)))
                    def _():
                        p_copy(k, ch).wait_send()

        for m in range(chips):
            x_copy(m).wait_send()
        for k in range(rows):
            for h in range(halves):
                if k == 0 and h == 0:
                    continue
                for d in range(1, cols):
                    y_copy(d, k, h).wait_send()
                if k < rows - 1:
                    z_copy(k, h).wait_send()
        for d in range(1, cols + 1):
            r_copy(d).wait_send()


def hand_over(low, anc, low_out, anc_out, sem):
    first = pltpu.make_async_copy(anc, anc_out, sem.at[0])
    second = pltpu.make_async_copy(low, low_out, sem.at[1])
    first.start()
    second.start()
    first.wait()
    second.wait()


def on_device(sizes, rhs_low, inv_low, blocks, targets, rhs_anc, inv_anc):
    layers, rows, cols = sizes
    levels, slots = blocks.shape[3], blocks.shape[4]
    width, cases = rhs_low.shape[3], rhs_low.shape[4]
    anc_row, narrow = rhs_anc.shape[0], rhs_anc.shape[2]
    share = cases // rows
    halves = 2 if anc_row % 2 == 0 else 1
    chips = rows // 2
    assert levels == 2 and layers == rows and layers % 2 == 0 and layers > 3 and cols <= rows
    assert cols * narrow == share
    any_space = pl.BlockSpec(memory_space=pltpu.HBM)
    dma = pltpu.SemaphoreType.DMA
    wide = anc_row * width // halves
    low, anc = pl.pallas_call(
        functools.partial(kernel, sizes),
        out_shape=(
            pltpu.VMEM((levels, width, share), BF16),
            pltpu.VMEM((anc_row, narrow, width), F32),
        ),
        in_specs=[any_space] * 6,
        out_specs=(pl.BlockSpec(memory_space=pltpu.VMEM), pl.BlockSpec(memory_space=pltpu.VMEM)),
        scratch_shapes=[
            pltpu.VMEM((levels, width, cases), BF16),
            pltpu.VMEM((levels, width, width), BF16),
            pltpu.VMEM((slots, width, width), BF16),
            pltpu.VMEM((slots, width, width), BF16),
            pltpu.VMEM((anc_row, narrow, width), BF16),
            pltpu.VMEM((anc_row, width, width), BF16),
            pltpu.VMEM((cases, width), BF16),
            pltpu.VMEM((rows, share, width), BF16),
            pltpu.VMEM((rows, share, width), BF16),
            pltpu.VMEM((chips, cols, share, width), BF16),
            pltpu.VMEM((cases, width), F32),
            pltpu.VMEM((cases, anc_row * width), F32),
            pltpu.VMEM((cols, rows, halves, narrow, wide), BF16),
            pltpu.VMEM((cols - 1, rows, halves, narrow, wide), BF16),
            pltpu.VMEM((rows - 1, halves, narrow, wide), BF16),
            pltpu.VMEM((layers + 1, halves, narrow, wide), BF16),
            pltpu.VMEM((2, cols, narrow, wide), BF16),
            pltpu.SMEM((levels, slots), jnp.int32),
            dma((9,)),
            dma((rows, chips)),
            dma((chips, cols)),
            dma((chips,)),
            dma((chips,)),
            dma((cols - 1, rows, halves)),
            dma((cols - 1, rows, halves)),
            dma((rows - 1, halves)),
            dma((layers + 1, halves)),
            dma((cols,)),
            dma((2, cols)),
        ],
        compiler_params=pltpu.CompilerParams(
            collective_id=0, has_side_effects=True, vmem_limit_bytes=56 * 1024 * 1024
        ),
    )(
        targets.reshape(levels, slots),
        rhs_low.reshape(levels, width, cases),
        inv_low.reshape(levels, width, width),
        blocks.reshape(levels, slots, width, width),
        rhs_anc.transpose(0, 2, 1),
        inv_anc,
    )
    low, anc = pl.pallas_call(
        hand_over,
        out_shape=(
            jax.ShapeDtypeStruct(low.shape, low.dtype),
            jax.ShapeDtypeStruct(anc.shape, anc.dtype),
        ),
        in_specs=[pl.BlockSpec(memory_space=pltpu.VMEM)] * 2,
        out_specs=(any_space, any_space),
        scratch_shapes=[dma((2,))],
        compiler_params=pltpu.CompilerParams(vmem_limit_bytes=4 * 1024 * 1024),
    )(low, anc)
    return low[None, :, None], anc.transpose(0, 2, 1)


def solution(mesh):
    sizes = tuple(mesh.shape[a] for a in ("layer", "row", "col"))
    in_specs = (
        P("layer", None, "col", None, None),
        P("layer", None, "col", None, None),
        P("layer", "row", "col", None, None, None, None),
        P("layer", "row", "col", None, None),
        P("row", None, ("layer", "col")),
        P("row", None, None),
    )
    out_specs = (P("layer", None, "col", None, "row"), P("row", None, ("layer", "col")))
    return jax.shard_map(
        functools.partial(on_device, sizes),
        mesh=mesh,
        in_specs=in_specs,
        out_specs=out_specs,
        check_vma=False,
    )
```

```python
import contextlib
import functools

import jax
import jax.numpy as jnp
from jax import lax
from jax.experimental import pallas as pl
from jax.experimental.pallas import tpu as pltpu
from jax.sharding import PartitionSpec as P

MESH = pl.DeviceIdType.MESH
F32 = jnp.float32
BF16 = jnp.bfloat16


def scope(name):
    return contextlib.nullcontext()


def dot_t(left, right):
    return lax.dot_general(left, right, (((1,), (1,)), ((), ())), preferred_element_type=F32)


def flag(condition):
    return condition.astype(jnp.int32)


def ranked(layer, layers):
    low = flag(layer < layers // 2)
    far, near = low * (layers - 1), (1 - low) * (layers - 1)
    keys = []
    for j in range(layers):
        key = -2 * layers * jnp.abs(layer - j) - j
        key = key - 1000 * layers * flag(far == j) + 1000 * layers * flag(near == j)
        keys.append(key + 5000 * layers * flag(layer == j))
    order = [0] * layers
    for j in range(layers):
        rank = 0
        for other in range(layers):
            if other != j:
                rank = rank + flag(keys[other] < keys[j])
        order = [order[k] + j * flag(rank == k) for k in range(layers)]
    return order


def kernel(
    sizes,
    targets_hbm,
    rhs_hbm,
    inv_hbm,
    blocks_hbm,
    rhs_anc_hbm,
    inv_anc_hbm,
    low_out,
    anc_out,
    rhs,
    inv,
    blocks0,
    blocks1,
    rhs_anc,
    inv_anc,
    x0,
    x1,
    part,
    part_in,
    rhs_t,
    base,
    packed,
    y_in,
    z_out,
    z_in,
    r_in,
    e_in,
    targets,
    load_sem,
    p_send,
    p_recv,
    x_send,
    x_recv,
    y_send,
    y_recv,
    z_send,
    z_recv,
    r_send,
    r_recv,
    e_send,
    e_recv,
):
    layers, rows, cols = sizes
    layer, row, col = (lax.axis_index(a) for a in ("layer", "row", "col"))
    slots = blocks0.shape[0]
    anc_row, narrow, width = rhs_anc.shape
    share = x1.shape[1]
    pieces = packed.shape[2]
    raw = pieces // 2
    chips = rows // 2
    last = layers - 1

    chip, core = row // 2, row % 2
    mate = row + 1 - 2 * core
    order = ranked(layer, layers)
    goal = (row + rows - 1) % rows
    active = goal < cols
    owner = (1 + col) % rows

    loads = [
        pltpu.make_async_copy(inv_hbm.at[0], inv.at[0], load_sem.at[0]),
        pltpu.make_async_copy(rhs_hbm.at[0], rhs.at[0], load_sem.at[1]),
        pltpu.make_async_copy(blocks_hbm.at[0], blocks0, load_sem.at[2]),
        pltpu.make_async_copy(inv_hbm.at[1], inv.at[1], load_sem.at[3]),
        pltpu.make_async_copy(rhs_hbm.at[1], rhs.at[1], load_sem.at[4]),
        pltpu.make_async_copy(blocks_hbm.at[1], blocks1, load_sem.at[5]),
        pltpu.make_async_copy(inv_anc_hbm, inv_anc, load_sem.at[6]),
        pltpu.make_async_copy(rhs_anc_hbm, rhs_anc, load_sem.at[7]),
        pltpu.make_async_copy(targets_hbm, targets, load_sem.at[8]),
    ]
    for n in (0, 1):
        loads[n].start()

    barrier = pltpu.get_barrier_semaphore()

    def greet(device):
        pl.semaphore_signal(barrier, inc=1, device_id=device, device_id_type=MESH)

    for d in range(1, rows):
        greet({"row": (row + d) % rows})
    for d in range(1, cols):
        greet({"col": (col + d) % cols})
    for step in (-1, 1):

        @pl.when(jnp.logical_and(layer + step >= 0, layer + step < layers))
        def _():
            greet({"layer": layer + step})

    for cc in range(cols):

        @pl.when(col != cc)
        def _():
            greet({"row": owner, "col": cc})

    @pl.when(jnp.logical_and(active, col != goal))
    def _():
        for r in range(rows):
            greet({"row": r, "col": goal})

    met = (rows - 1) + (cols - 1) + flag(layer > 0) + flag(layer < last)
    met = met + (cols - 1) + flag(jnp.logical_and(active, col != goal)) * rows

    for n in (8, 2, 3, 4, 5, 6, 7):
        loads[n].start()

    def listed(level, target):
        index, found = jnp.int32(0), jnp.int32(0)
        for s in range(slots):
            hit = (targets[level, s] == target).astype(jnp.int32)
            index = index + hit * s
            found = found + hit
        return (blocks0, blocks1)[level][index], found.astype(F32)

    def span(j):
        return pl.ds(pl.multiple_of(j * share, share), share)

    def solver(k, source):
        if k < 2:
            return [2 * ch + k for ch in range(chips)]
        return [2 * ((source // 2 + k - 2) % chips)]

    def place(k):
        return 0 if k < 2 else 1 + (k - 2) // chips

    def p_copy(k, n):
        return pltpu.make_async_remote_copy(
            src_ref=part.at[k],
            dst_ref=part_in.at[place(k), col],
            send_sem=p_send.at[k, n],
            recv_sem=p_recv.at[place(k), col],
            device_id={"row": solver(k, row)[n], "col": goal},
            device_id_type=MESH,
        )

    def here(k, n):
        return jnp.logical_and(goal == col, row == solver(k, row)[n])

    def part_of(k):
        block, found = listed(0, 1)
        part[k] = (dot_t(x0[span(order[k]), :], block) * found).astype(BF16)

    def part_out(k):
        for n in range(len(solver(k, row))):

            @pl.when(jnp.logical_not(here(k, n)))
            def _():
                p_copy(k, n).start()

            @pl.when(here(k, n))
            def _():
                part_in[place(k), col] = part[k]

    def lower(k):
        if share % 128 == 0:
            first = jnp.dot(inv[0], rhs[0, :, span(order[k])], preferred_element_type=F32)
            x0[span(order[k]), :] = first.T.astype(BF16)
        elif k == 0:
            first = jnp.dot(inv[0], rhs[0], preferred_element_type=F32)
            x0[...] = first.T.astype(BF16)

    with scope("ldx0"):
        loads[0].wait()
        loads[1].wait()
    with scope("x0"):
        lower(0)
    loads[8].wait()
    loads[2].wait()

    @pl.when(active)
    def _():
        part_of(0)

    with scope("barr"):
        pl.semaphore_wait(barrier, met)

    with scope("part"):

        @pl.when(active)
        def _():
            part_out(0)
            for k in range(1, rows):
                lower(k)
                part_of(k)
                part_out(k)

        @pl.when(jnp.logical_not(active))
        def _():
            for k in range(1, rows):
                lower(k)

    loads[3].wait()
    loads[4].wait()
    rhs_t[...] = rhs[1].astype(F32).T

    with scope("base"):
        for a in range(anc_row):
            block, found = listed(0, a + 2)
            base[:, a * width : (a + 1) * width] = dot_t(x0[...], block) * found

    for j in range(rows):

        @pl.when(row == j)
        def _():
            low_out[0] = x0[j * share : (j + 1) * share, :].astype(F32).T.astype(BF16)

    for edge, one, two in ((0, 0, layers), (last, layers, last)):

        @pl.when(layer == edge)
        def _():
            for h in range(pieces):
                if h < raw:
                    z_in[one, h] = jnp.zeros_like(z_in[one, h])
                elif layers == 4:
                    z_in[two, h] = jnp.zeros_like(z_in[two, h])

    loads[5].wait()

    def mate_copy(k):
        return pltpu.make_async_remote_copy(
            src_ref=x1.at[order[k]],
            dst_ref=x1.at[order[k]],
            send_sem=x_send.at[k, 0],
            recv_sem=x_recv.at[k],
            device_id={"row": mate},
            device_id_type=MESH,
        )

    def x_copy(k, d):
        return pltpu.make_async_remote_copy(
            src_ref=x1.at[order[k]],
            dst_ref=x1.at[order[k]],
            send_sem=x_send.at[k, d - 1],
            recv_sem=x_recv.at[k],
            device_id={"row": (row + d) % rows},
            device_id_type=MESH,
        )

    def solve(k):
        for cc in range(cols):

            @pl.when(jnp.logical_or(col != cc, row != owner))
            def _():
                pltpu.make_async_remote_copy(
                    src_ref=part.at[0],
                    dst_ref=part_in.at[place(k), cc],
                    send_sem=p_send.at[0, 0],
                    recv_sem=p_recv.at[place(k), cc],
                    device_id={"row": mate},
                    device_id_type=MESH,
                ).wait_recv()

        total = part_in[place(k), 0].astype(F32)
        for cc in range(1, cols):
            total = total + part_in[place(k), cc].astype(F32)
        residual = (rhs_t[span(order[k]), :] - total).astype(BF16)
        x1[order[k]] = dot_t(residual, inv[1]).astype(BF16)

    def solve_all(k):
        @pl.when(row == solver(k, owner)[0])
        def _():
            solve(k)
            for d in range(1, rows):
                x_copy(k, d).start()

    def y_copy(d, k, h):
        cc = (col + d) % cols
        return pltpu.make_async_remote_copy(
            src_ref=packed.at[cc, k, h],
            dst_ref=y_in.at[d - 1, k, h],
            send_sem=y_send.at[d - 1, k, h],
            recv_sem=y_recv.at[d - 1, k, h],
            device_id={"col": cc},
            device_id_type=MESH,
        )

    def products(k):
        @pl.when(core != k if k < 2 else row != solver(k, owner)[0])
        def _():
            mate_copy(k).wait_recv()

        j = order[k]
        for a in range(anc_row):
            block, found = listed(1, a + 2)
            at = slice(a * width, (a + 1) * width)
            value = base[span(j), at] + dot_t(x1[j], block) * found
            value = value.astype(BF16)
            for cc in range(cols):
                packed[cc, k, a] = value[cc * narrow : (cc + 1) * narrow]
            sent(k, a)

    end = jnp.logical_or(layer == 0, layer == last)
    middle = jnp.logical_or(layer == layers // 2 - 1, layer == layers // 2)
    upper = layer == layers // 2
    beside = jnp.logical_or(layer == layers // 2 - 2, layer == layers // 2 + 1)
    onward = layer + 2 * flag(order[0] > layer) - 1

    others, whole = range(1, cols), range(1, cols + 1)

    def sent(k, h):
        if k == 0 and h < raw:

            @pl.when(end)
            def _():
                for d in others:
                    r_copy(d, h).start()
                if h == raw - 1:
                    for n in range(raw):
                        r_copy(cols, n).start()

        elif k == rows - 2 and h >= raw:

            @pl.when(middle)
            def _():
                for d in others:
                    e_copy(d, h).start()
                if h == pieces - 1:
                    for n in range(raw, pieces):
                        e_copy(cols, n).start()

            @pl.when(jnp.logical_not(middle))
            def _():
                exchange(k, h)

        elif k == rows - 2:

            @pl.when(jnp.logical_not(middle))
            def _():
                exchange(k, h)

        elif k == rows - 1:

            @pl.when(jnp.logical_not(jnp.logical_or(middle, end) if h >= raw else middle))
            def _():
                exchange(k, h)

        else:
            exchange(k, h)

    def exchange(k, h):
        for d in range(1, cols):
            y_copy(d, k, h).start()

    def r_copy(d, h):
        cc = (col + d) % cols
        return pltpu.make_async_remote_copy(
            src_ref=packed.at[cc, 0, h],
            dst_ref=r_in.at[flag(middle), d - 1, h],
            send_sem=r_send.at[d - 1, h],
            recv_sem=r_recv.at[flag(middle), d - 1, h],
            device_id={"layer": onward},
            device_id_type=MESH,
        )

    def r_add(slot, k, d, h):
        pltpu.make_async_remote_copy(
            src_ref=packed.at[col, 0, h],
            dst_ref=r_in.at[slot, d - 1, h],
            send_sem=r_send.at[d - 1, h],
            recv_sem=r_recv.at[slot, d - 1, h],
            device_id={"layer": onward},
            device_id_type=MESH,
        ).wait_recv()
        cc = (col + d) % cols
        value = packed[cc, k, h].astype(F32) + r_in[slot, d - 1, h].astype(F32)
        packed[cc, k, h] = value.astype(BF16)

    def e_copy(d, h):
        cc = (col + d) % cols
        return pltpu.make_async_remote_copy(
            src_ref=packed.at[cc, rows - 2, h],
            dst_ref=e_in.at[d - 1, h - raw],
            send_sem=e_send.at[d - 1, h - raw],
            recv_sem=e_recv.at[d - 1, h - raw],
            device_id={"layer": order[rows - 2]},
            device_id_type=MESH,
        )

    def e_add(d, h):
        e_copy(d, h).wait_recv()
        cc = (col + d) % cols
        value = packed[cc, rows - 1, h].astype(F32) + e_in[d - 1, h - raw].astype(F32)
        packed[cc, rows - 1, h] = value.astype(BF16)

    def z_copy(k, h):
        j = order[k]
        toward = layer + 2 * flag(j > layer) - 1
        slot = j + flag(j == layer - 1) * (layers - j)
        if k == 0:
            toward = toward + flag(middle) * (j - toward)
            slot = slot + flag(middle) * flag(j == last) * (layers - slot)
        return pltpu.make_async_remote_copy(
            src_ref=z_out.at[k, h],
            dst_ref=z_in.at[slot, h],
            send_sem=z_send.at[k, h],
            recv_sem=z_recv.at[slot, h],
            device_id={"layer": toward},
            device_id_type=MESH,
        )

    def z_wait(slot, h):
        pltpu.make_async_remote_copy(
            src_ref=z_out.at[0, h],
            dst_ref=z_in.at[slot, h],
            send_sem=z_send.at[0, h],
            recv_sem=z_recv.at[slot, h],
            device_id={"layer": (layer + 1) % layers},
            device_id_type=MESH,
        ).wait_recv()

    def merged(k, h):
        for d in range(1, cols):
            y_copy(d, k, h).wait_recv()
        value = packed[col, k, h].astype(F32)
        for d in range(1, cols):
            value = value + y_in[d - 1, k, h].astype(F32)
        return value

    def merge(k, h):
        with scope("y%d%d" % (k, h)):
            value = merged(k, h)
        j = order[k]
        passing = jnp.logical_or(
            jnp.logical_and(j > layer, layer > 0), jnp.logical_and(j < layer, layer < last)
        )
        if k == rows - 2:
            passing = jnp.logical_and(passing, jnp.logical_not(middle))
            if h >= raw:
                passing = jnp.logical_and(passing, jnp.logical_not(beside))

        with scope("z%d%d" % (k, h)):

            @pl.when(passing)
            def _():
                z_wait(j, h)
                z_out[k, h] = (value + z_in[j, h].astype(F32)).astype(BF16)

            @pl.when(jnp.logical_not(passing))
            def _():
                z_out[k, h] = value.astype(BF16)

        z_copy(k, h).start()

    for k in range(2):

        @pl.when(core == k)
        def _():
            with scope("x1"):
                solve(k)
            mate_copy(k).start()

    first = [(0, h) for h in range(raw, pieces)]
    early = [(k, h) for k in range(1, rows - 2) for h in range(pieces)]
    late = [(rows - 2, h) for h in range(pieces)]

    for k in range(rows):
        with scope("p%d" % k):
            products(k)
        if k == 0:
            with scope("x1_2"):
                solve_all(2)
        elif k == 1:
            with scope("x1_3"):
                for other in range(3, rows):
                    solve_all(other)

            @pl.when(jnp.logical_not(end))
            def _():
                with scope("rf1"):
                    for h in range(raw):
                        for d in others:
                            r_add(0, 0, d, h)
                            r_copy(d, h).start()

        elif k == 2:

            @pl.when(end)
            def _():
                for k, h in first:
                    merge(k, h)

            @pl.when(jnp.logical_not(end))
            def _():
                with scope("rf2"):
                    for h in range(raw):
                        r_add(0, 0, cols, h)
                        r_copy(cols, h).start()

    low_out[1] = x1[row].astype(F32).T.astype(BF16)

    @pl.when(middle)
    def _():
        with scope("rn"):
            for h in range(raw):
                for d in others:
                    r_add(1, rows - 2, d, h)
                exchange(rows - 2, h)
            for h in range(pieces):
                exchange(rows - 1, h)

        for k, h in first:
            merge(k, h)

        with scope("rw"):
            for h in range(raw):
                r_add(1, rows - 2, cols, h)

        near = late[:raw]

        @pl.when(upper)
        def _():
            for k, h in early[:-2] + near + early[-2:]:
                merge(k, h)

        @pl.when(jnp.logical_not(upper))
        def _():
            for k, h in early[:-1] + near[:1] + early[-1:] + near[1:]:
                merge(k, h)

    @pl.when(jnp.logical_not(middle))
    def _():
        @pl.when(jnp.logical_not(end))
        def _():
            for k, h in first:
                merge(k, h)

        for k, h in early + late[:raw]:
            merge(k, h)

        with scope("e"):

            @pl.when(end)
            def _():
                for h in range(raw, pieces):
                    for d in others:
                        e_add(d, h)
                    exchange(rows - 1, h)
                for h in range(raw, pieces):
                    e_add(cols, h)

        for k, h in late[raw:]:
            merge(k, h)

    loads[6].wait()
    loads[7].wait()
    for h in range(pieces):
        with scope("zown%d" % h):
            for slot, edge, far in ((layer, 0, last), (layers, last, 0)):
                if h < raw:

                    @pl.when(layer != edge)
                    def _():
                        z_wait(slot, h)

                elif layers == 4:

                    @pl.when(layer != far)
                    def _():
                        z_wait(slot, h)

                else:
                    z_wait(slot, h)

        with scope("yown%d" % h):
            value = merged(rows - 1, h)
        with scope("fin%d" % h):
            value = value + z_in[layer, h].astype(F32) + z_in[layers, h].astype(F32)
            residual = (rhs_anc[h].astype(F32) - value).astype(BF16)
            anc_out[h] = dot_t(residual, inv_anc[h])

    with scope("sent"):

        @pl.when(active)
        def _():
            for k in range(rows):
                for n in range(len(solver(k, row))):

                    @pl.when(jnp.logical_not(here(k, n)))
                    def _():
                        p_copy(k, n).wait_send()

        for k in range(2):

            @pl.when(core == k)
            def _():
                mate_copy(k).wait_send()

        for k in range(2, rows):

            @pl.when(row == solver(k, owner)[0])
            def _():
                for d in range(1, rows):
                    x_copy(k, d).wait_send()

        for k in range(rows):
            for h in range(pieces):
                if k == 0 and h < raw or k == rows - 2 and h >= raw:
                    continue
                for d in others:
                    y_copy(d, k, h).wait_send()
                if k < rows - 1:
                    z_copy(k, h).wait_send()
        for d in whole:
            for h in range(raw):
                r_copy(d, h).wait_send()

        for h in range(raw, pieces):

            @pl.when(middle)
            def _():
                for d in whole:
                    e_copy(d, h).wait_send()

            @pl.when(jnp.logical_not(middle))
            def _():
                for d in others:
                    y_copy(d, rows - 2, h).wait_send()
                z_copy(rows - 2, h).wait_send()


def hand_over(low, anc, low_out, anc_out, sem):
    first = pltpu.make_async_copy(anc, anc_out, sem.at[0])
    second = pltpu.make_async_copy(low, low_out, sem.at[1])
    first.start()
    second.start()
    first.wait()
    second.wait()


def on_device(sizes, rhs_low, inv_low, blocks, targets, rhs_anc, inv_anc):
    layers, rows, cols = sizes
    levels, slots = blocks.shape[3], blocks.shape[4]
    width, cases = rhs_low.shape[3], rhs_low.shape[4]
    anc_row, narrow = rhs_anc.shape[0], rhs_anc.shape[2]
    share = cases // rows
    pieces, raw = anc_row, anc_row // 2
    chips = rows // 2
    places = 1 + pl.cdiv(rows - 2, chips)
    assert levels == 2 and layers == rows and layers % 2 == 0 and layers > 3 and cols <= rows
    assert cols * narrow == share and anc_row % 2 == 0
    any_space = pl.BlockSpec(memory_space=pltpu.HBM)
    dma = pltpu.SemaphoreType.DMA
    low, anc = pl.pallas_call(
        functools.partial(kernel, sizes),
        out_shape=(
            pltpu.VMEM((levels, width, share), BF16),
            pltpu.VMEM((anc_row, narrow, width), F32),
        ),
        in_specs=[any_space] * 6,
        out_specs=(pl.BlockSpec(memory_space=pltpu.VMEM), pl.BlockSpec(memory_space=pltpu.VMEM)),
        scratch_shapes=[
            pltpu.VMEM((levels, width, cases), BF16),
            pltpu.VMEM((levels, width, width), BF16),
            pltpu.VMEM((slots, width, width), BF16),
            pltpu.VMEM((slots, width, width), BF16),
            pltpu.VMEM((anc_row, narrow, width), BF16),
            pltpu.VMEM((anc_row, width, width), BF16),
            pltpu.VMEM((cases, width), BF16),
            pltpu.VMEM((rows, share, width), BF16),
            pltpu.VMEM((rows, share, width), BF16),
            pltpu.VMEM((places, cols, share, width), BF16),
            pltpu.VMEM((cases, width), F32),
            pltpu.VMEM((cases, anc_row * width), F32),
            pltpu.VMEM((cols, rows, pieces, narrow, width), BF16),
            pltpu.VMEM((cols - 1, rows, pieces, narrow, width), BF16),
            pltpu.VMEM((rows - 1, pieces, narrow, width), BF16),
            pltpu.VMEM((layers + 1, pieces, narrow, width), BF16),
            pltpu.VMEM((2, cols, raw, narrow, width), BF16),
            pltpu.VMEM((cols, pieces - raw, narrow, width), BF16),
            pltpu.SMEM((levels, slots), jnp.int32),
            dma((9,)),
            dma((rows, chips)),
            dma((places, cols)),
            dma((rows, rows - 1)),
            dma((rows,)),
            dma((cols - 1, rows, pieces)),
            dma((cols - 1, rows, pieces)),
            dma((rows - 1, pieces)),
            dma((layers + 1, pieces)),
            dma((cols, raw)),
            dma((2, cols, raw)),
            dma((cols, pieces - raw)),
            dma((cols, pieces - raw)),
        ],
        compiler_params=pltpu.CompilerParams(
            collective_id=0, has_side_effects=True, vmem_limit_bytes=56 * 1024 * 1024
        ),
    )(
        targets.reshape(levels, slots),
        rhs_low.reshape(levels, width, cases),
        inv_low.reshape(levels, width, width),
        blocks.reshape(levels, slots, width, width),
        rhs_anc.transpose(0, 2, 1),
        inv_anc,
    )
    low, anc = pl.pallas_call(
        hand_over,
        out_shape=(
            jax.ShapeDtypeStruct(low.shape, low.dtype),
            jax.ShapeDtypeStruct(anc.shape, anc.dtype),
        ),
        in_specs=[pl.BlockSpec(memory_space=pltpu.VMEM)] * 2,
        out_specs=(any_space, any_space),
        scratch_shapes=[dma((2,))],
        compiler_params=pltpu.CompilerParams(vmem_limit_bytes=4 * 1024 * 1024),
    )(low, anc)
    return low[None, :, None], anc.transpose(0, 2, 1)


def solution(mesh):
    sizes = tuple(mesh.shape[a] for a in ("layer", "row", "col"))
    in_specs = (
        P("layer", None, "col", None, None),
        P("layer", None, "col", None, None),
        P("layer", "row", "col", None, None, None, None),
        P("layer", "row", "col", None, None),
        P("row", None, ("layer", "col")),
        P("row", None, None),
    )
    out_specs = (P("layer", None, "col", None, "row"), P("row", None, ("layer", "col")))
    return jax.shard_map(
        functools.partial(on_device, sizes),
        mesh=mesh,
        in_specs=in_specs,
        out_specs=out_specs,
        check_vma=False,
    )
```

```python
import contextlib
import functools

import jax
import jax.numpy as jnp
from jax import lax
from jax.experimental import pallas as pl
from jax.experimental.pallas import tpu as pltpu
from jax.sharding import PartitionSpec as P

MESH = pl.DeviceIdType.MESH
F32 = jnp.float32
BF16 = jnp.bfloat16


def scope(name):
    return contextlib.nullcontext()


def dot_t(left, right):
    return lax.dot_general(left, right, (((1,), (1,)), ((), ())), preferred_element_type=F32)


def flag(condition):
    return condition.astype(jnp.int32)


def ranked(layer, layers):
    low = flag(layer < layers // 2)
    far, near = low * (layers - 1), (1 - low) * (layers - 1)
    keys = []
    for j in range(layers):
        key = -2 * layers * jnp.abs(layer - j) - j
        key = key - 1000 * layers * flag(far == j) + 1000 * layers * flag(near == j)
        keys.append(key + 5000 * layers * flag(layer == j))
    order = [0] * layers
    for j in range(layers):
        rank = 0
        for other in range(layers):
            if other != j:
                rank = rank + flag(keys[other] < keys[j])
        order = [order[k] + j * flag(rank == k) for k in range(layers)]
    return order


def kernel(
    sizes,
    targets_hbm,
    rhs_hbm,
    inv_hbm,
    blocks_hbm,
    rhs_anc_hbm,
    inv_anc_hbm,
    low_out,
    anc_out,
    rhs,
    inv,
    blocks0,
    blocks1,
    rhs_anc,
    inv_anc,
    x0,
    x1,
    part,
    part_in,
    rhs_t,
    base,
    packed,
    y_in,
    z_out,
    z_in,
    r_in,
    e_in,
    targets,
    load_sem,
    p_send,
    p_recv,
    x_send,
    x_recv,
    y_recv,
    z_recv,
    r_recv,
    e_recv,
    send_sem,
):
    layers, rows, cols = sizes
    layer, row, col = (lax.axis_index(a) for a in ("layer", "row", "col"))
    slots = blocks0.shape[0]
    anc_row, narrow, width = rhs_anc.shape
    share = x1.shape[1]
    pieces = anc_row
    raw = pieces // 2
    chips = rows // 2
    last = layers - 1

    chip, core = row // 2, row % 2
    mate = row + 1 - 2 * core
    order = ranked(layer, layers)
    goal = (row + rows - 1) % rows
    active = goal < cols
    owner = (1 + col) % rows

    loads = [
        pltpu.make_async_copy(inv_hbm.at[0], inv.at[0], load_sem.at[0]),
        pltpu.make_async_copy(rhs_hbm.at[0], rhs.at[0], load_sem.at[1]),
        pltpu.make_async_copy(blocks_hbm.at[0], blocks0, load_sem.at[2]),
        pltpu.make_async_copy(inv_hbm.at[1], inv.at[1], load_sem.at[3]),
        pltpu.make_async_copy(rhs_hbm.at[1], rhs.at[1], load_sem.at[4]),
        pltpu.make_async_copy(blocks_hbm.at[1], blocks1, load_sem.at[5]),
        pltpu.make_async_copy(inv_anc_hbm, inv_anc, load_sem.at[6]),
        pltpu.make_async_copy(rhs_anc_hbm, rhs_anc, load_sem.at[7]),
        pltpu.make_async_copy(targets_hbm, targets, load_sem.at[8]),
    ]
    for n in (0, 1):
        loads[n].start()

    barrier = pltpu.get_barrier_semaphore()

    def greet(device):
        pl.semaphore_signal(barrier, inc=1, device_id=device, device_id_type=MESH)

    for d in range(1, rows):
        greet({"row": (row + d) % rows})
    for d in range(1, cols):
        greet({"col": (col + d) % cols})
    for step in (-1, 1):

        @pl.when(jnp.logical_and(layer + step >= 0, layer + step < layers))
        def _():
            greet({"layer": layer + step})

    for cc in range(cols):

        @pl.when(col != cc)
        def _():
            greet({"row": owner, "col": cc})

    @pl.when(jnp.logical_and(active, col != goal))
    def _():
        for r in range(rows):
            greet({"row": r, "col": goal})

    met = (rows - 1) + (cols - 1) + flag(layer > 0) + flag(layer < last)
    met = met + (cols - 1) + flag(jnp.logical_and(active, col != goal)) * rows

    for n in (8, 2, 3, 4, 5, 6, 7):
        loads[n].start()

    def spare(j):
        return (1 - j % 2) * last if layers == 4 else layers

    def at(cc, k, h):
        return (cc * rows + k) * pieces + h

    def sends(n):
        return pltpu.make_async_remote_copy(
            src_ref=packed.at[0:n],
            dst_ref=packed.at[0:n],
            send_sem=send_sem,
            recv_sem=send_sem,
            device_id={"row": mate},
            device_id_type=MESH,
        )

    def listed(level, target):
        index, found = jnp.int32(0), jnp.int32(0)
        for s in range(slots):
            hit = (targets[level, s] == target).astype(jnp.int32)
            index = index + hit * s
            found = found + hit
        return (blocks0, blocks1)[level][index], found.astype(F32)

    def span(j):
        return pl.ds(pl.multiple_of(j * share, share), share)

    def solver(k, source):
        if k < 2:
            return [2 * ch + k for ch in range(chips)]
        return [2 * ((source // 2 + k - 2) % chips)]

    def place(k):
        return 0 if k < 2 else 1 + (k - 2) // chips

    def p_copy(k, n):
        return pltpu.make_async_remote_copy(
            src_ref=part.at[k],
            dst_ref=part_in.at[place(k), col],
            send_sem=p_send,
            recv_sem=p_recv.at[place(k), col],
            device_id={"row": solver(k, row)[n], "col": goal},
            device_id_type=MESH,
        )

    def here(k, n):
        return jnp.logical_and(goal == col, row == solver(k, row)[n])

    def part_of(k):
        block, found = listed(0, 1)
        part[k] = (dot_t(x0[span(order[k]), :], block) * found).astype(BF16)

    def part_out(k):
        for n in range(len(solver(k, row))):

            @pl.when(jnp.logical_not(here(k, n)))
            def _():
                p_copy(k, n).start()

            @pl.when(here(k, n))
            def _():
                part_in[place(k), col] = part[k]

    def lower(k):
        if share % 128 == 0:
            first = jnp.dot(inv[0], rhs[0, :, span(order[k])], preferred_element_type=F32)
            x0[span(order[k]), :] = first.T.astype(BF16)
        elif k == 0:
            first = jnp.dot(inv[0], rhs[0], preferred_element_type=F32)
            x0[...] = first.T.astype(BF16)

    with scope("ldx0"):
        loads[0].wait()
        loads[1].wait()
    with scope("x0"):
        lower(0)
    loads[8].wait()
    loads[2].wait()

    @pl.when(active)
    def _():
        part_of(0)

    with scope("barr"):
        pl.semaphore_wait(barrier, met)

    with scope("part"):

        @pl.when(active)
        def _():
            part_out(0)
            for k in range(1, rows):
                lower(k)
                part_of(k)
                part_out(k)

        @pl.when(jnp.logical_not(active))
        def _():
            for k in range(1, rows):
                lower(k)

    loads[3].wait()
    loads[4].wait()
    rhs_t[...] = rhs[1].astype(F32).T

    with scope("base"):
        for a in range(anc_row):
            block, found = listed(0, a + 2)
            base[:, a * width : (a + 1) * width] = dot_t(x0[...], block) * found

    for j in range(rows):

        @pl.when(row == j)
        def _():
            low_out[0] = x0[j * share : (j + 1) * share, :].astype(F32).T.astype(BF16)

    for edge, one, two in ((0, 0, spare(0)), (last, spare(last), last)):

        @pl.when(layer == edge)
        def _():
            for h in range(pieces):
                if h < raw:
                    z_in[one, h] = jnp.zeros_like(z_in[one, h])
                elif layers == 4:
                    z_in[two, h] = jnp.zeros_like(z_in[two, h])

    loads[5].wait()

    def mate_copy(k):
        return pltpu.make_async_remote_copy(
            src_ref=x1.at[order[k]],
            dst_ref=x1.at[order[k]],
            send_sem=x_send.at[0],
            recv_sem=x_recv.at[k],
            device_id={"row": mate},
            device_id_type=MESH,
        )

    def x_copy(k, d):
        return pltpu.make_async_remote_copy(
            src_ref=x1.at[order[k]],
            dst_ref=x1.at[order[k]],
            send_sem=x_send.at[k - 1],
            recv_sem=x_recv.at[k],
            device_id={"row": (row + d) % rows},
            device_id_type=MESH,
        )

    def p_sent(n):
        pltpu.make_async_remote_copy(
            src_ref=packed.at[0 : n * cols],
            dst_ref=packed.at[0 : n * cols],
            send_sem=p_send,
            recv_sem=p_send,
            device_id={"row": mate},
            device_id_type=MESH,
        ).wait_send()

    def x_sent(k):
        pltpu.make_async_remote_copy(
            src_ref=x1.at[0 : rows - 1],
            dst_ref=x1.at[0 : rows - 1],
            send_sem=x_send.at[k - 1],
            recv_sem=x_send.at[k - 1],
            device_id={"row": mate},
            device_id_type=MESH,
        ).wait_send()

    def solve(k):
        for cc in range(cols):

            @pl.when(jnp.logical_or(col != cc, row != owner))
            def _():
                pltpu.make_async_remote_copy(
                    src_ref=part.at[0],
                    dst_ref=part_in.at[place(k), cc],
                    send_sem=p_send,
                    recv_sem=p_recv.at[place(k), cc],
                    device_id={"row": mate},
                    device_id_type=MESH,
                ).wait_recv()

        total = part_in[place(k), 0].astype(F32)
        for cc in range(1, cols):
            total = total + part_in[place(k), cc].astype(F32)
        residual = (rhs_t[span(order[k]), :] - total).astype(BF16)
        x1[order[k]] = dot_t(residual, inv[1]).astype(BF16)

    def solve_all(k):
        @pl.when(row == solver(k, owner)[0])
        def _():
            solve(k)
            for d in range(1, rows):
                x_copy(k, d).start()

    def y_copy(d, k, h):
        cc = (col + d) % cols
        return pltpu.make_async_remote_copy(
            src_ref=packed.at[at(cc, k, h)],
            dst_ref=y_in.at[d - 1, k, h],
            send_sem=send_sem,
            recv_sem=y_recv.at[d - 1, k * pieces + h - raw],
            device_id={"col": cc},
            device_id_type=MESH,
        )

    others, whole = range(1, cols), range(1, cols + 1)
    mixed = [(h, h + raw) for h in range(raw)]
    plain = [(2 * h, 2 * h + 1) for h in range(raw)]

    def products(k):
        @pl.when(core != k if k < 2 else row != solver(k, owner)[0])
        def _():
            mate_copy(k).wait_recv()

        j = order[k]
        for pair in plain if k else mixed:
            for a in pair:
                block, found = listed(1, a + 2)
                lanes = slice(a * width, (a + 1) * width)
                value = base[span(j), lanes] + dot_t(x1[j], block) * found
                value = value.astype(BF16)
                for cc in range(cols):
                    packed[at(cc, k, a)] = value[cc * narrow : (cc + 1) * narrow]
            for a in pair:
                sent(k, a)

    end = jnp.logical_or(layer == 0, layer == last)
    middle = jnp.logical_or(layer == layers // 2 - 1, layer == layers // 2)
    upper = layer == layers // 2
    beside = jnp.logical_or(layer == layers // 2 - 2, layer == layers // 2 + 1)
    onward = layer + 2 * flag(order[0] > layer) - 1


    def sent(k, h):
        if k == 0 and h < raw:

            @pl.when(end)
            def _():
                for d in others:
                    r_copy(d, h).start()
                if h == raw - 1:
                    for n in range(raw):
                        r_copy(cols, n).start()

        elif k == rows - 2 and h >= raw:

            @pl.when(middle)
            def _():
                for d in others:
                    e_copy(d, h).start()
                if h == pieces - 1:
                    for n in range(raw, pieces):
                        e_copy(cols, n).start()

            @pl.when(jnp.logical_not(middle))
            def _():
                exchange(k, h)

        elif k == rows - 2:

            @pl.when(jnp.logical_not(middle))
            def _():
                exchange(k, h)

        elif k == rows - 1:

            if h < raw:
                exchange(k, h)
            else:

                @pl.when(jnp.logical_not(end))
                def _():
                    exchange(k, h)

        else:
            exchange(k, h)

    def exchange(k, h):
        for d in range(1, cols):
            y_copy(d, k, h).start()

    def r_place(d, h):
        return (d - 1) * raw + h if d < cols else (cols - 1) * raw

    def e_place(d, h):
        return (d - 1) * (pieces - raw) + h - raw if d < cols else (cols - 1) * (pieces - raw)

    def r_copy(d, h):
        cc = (col + d) % cols
        return pltpu.make_async_remote_copy(
            src_ref=packed.at[at(cc, 0, h)],
            dst_ref=r_in.at[flag(middle), d - 1, h],
            send_sem=send_sem,
            recv_sem=r_recv.at[flag(middle), r_place(d, h)],
            device_id={"layer": onward},
            device_id_type=MESH,
        )

    def r_wait(slot, d, h):
        own = d == cols
        pltpu.make_async_remote_copy(
            src_ref=r_in.at[slot, d - 1] if own else r_in.at[slot, d - 1, h],
            dst_ref=r_in.at[slot, d - 1] if own else r_in.at[slot, d - 1, h],
            send_sem=send_sem,
            recv_sem=r_recv.at[slot, r_place(d, h)],
            device_id={"layer": onward},
            device_id_type=MESH,
        ).wait_recv()

    def r_add(slot, k, d, h):
        if d < cols or h == 0:
            r_wait(slot, d, h)
        cc = (col + d) % cols
        value = packed[at(cc, k, h)].astype(F32) + r_in[slot, d - 1, h].astype(F32)
        packed[at(cc, k, h)] = value.astype(BF16)

    def e_copy(d, h):
        cc = (col + d) % cols
        return pltpu.make_async_remote_copy(
            src_ref=packed.at[at(cc, rows - 2, h)],
            dst_ref=e_in.at[d - 1, h - raw],
            send_sem=send_sem,
            recv_sem=e_recv.at[e_place(d, h)],
            device_id={"layer": order[rows - 2]},
            device_id_type=MESH,
        )

    def e_add(d, h):
        if d < cols:
            e_copy(d, h).wait_recv()
        elif h == raw:
            pltpu.make_async_remote_copy(
                src_ref=e_in.at[d - 1],
                dst_ref=e_in.at[d - 1],
                send_sem=send_sem,
                recv_sem=e_recv.at[e_place(d, h)],
                device_id={"layer": onward},
                device_id_type=MESH,
            ).wait_recv()
        cc = (col + d) % cols
        value = packed[at(cc, rows - 1, h)].astype(F32) + e_in[d - 1, h - raw].astype(F32)
        packed[at(cc, rows - 1, h)] = value.astype(BF16)

    def z_copy(k, h):
        j = order[k]
        toward = layer + 2 * flag(j > layer) - 1
        if k == 0:
            toward = toward + flag(middle) * (j - toward)
        other = jnp.logical_and(j == toward, j < layer)
        if k == 0:
            other = jnp.logical_and(j == toward, jnp.logical_xor(j < layer, middle))
        slot = j + flag(other) * (spare(j) - j)
        return pltpu.make_async_remote_copy(
            src_ref=z_out.at[k, h],
            dst_ref=z_in.at[slot, h],
            send_sem=send_sem,
            recv_sem=z_recv.at[slot, h],
            device_id={"layer": toward},
            device_id_type=MESH,
        )

    def z_wait(slot, h):
        pltpu.make_async_remote_copy(
            src_ref=z_out.at[0, h],
            dst_ref=z_in.at[slot, h],
            send_sem=send_sem,
            recv_sem=z_recv.at[slot, h],
            device_id={"layer": (layer + 1) % layers},
            device_id_type=MESH,
        ).wait_recv()

    def merged(k, h):
        for d in range(1, cols):
            y_copy(d, k, h).wait_recv()
        value = packed[at(col, k, h)].astype(F32)
        for d in range(1, cols):
            value = value + y_in[d - 1, k, h].astype(F32)
        return value

    def merge(k, h):
        with scope("y%d%d" % (k, h)):
            value = merged(k, h)
        j = order[k]
        passing = jnp.logical_or(
            jnp.logical_and(j > layer, layer > 0), jnp.logical_and(j < layer, layer < last)
        )
        if k == rows - 2:
            passing = jnp.logical_and(passing, jnp.logical_not(middle))
            if h >= raw:
                passing = jnp.logical_and(passing, jnp.logical_not(beside))

        with scope("z%d%d" % (k, h)):

            @pl.when(passing)
            def _():
                z_wait(j, h)
                z_out[k, h] = (value + z_in[j, h].astype(F32)).astype(BF16)

            @pl.when(jnp.logical_not(passing))
            def _():
                z_out[k, h] = value.astype(BF16)

        z_copy(k, h).start()

    for k in range(2):

        @pl.when(core == k)
        def _():
            with scope("x1"):
                solve(k)
            mate_copy(k).start()

    first = [(0, h) for h in range(raw, pieces)]
    early = [(k, h) for k in range(1, rows - 2) for h in range(pieces)]
    late = [(rows - 2, h) for h in range(pieces)]

    def step(k):
        with scope("p%d" % k):
            products(k)

    step(0)
    with scope("x1_2"):
        solve_all(2)
    step(1)
    with scope("x1_3"):
        for k in range(3, rows):
            solve_all(k)

    @pl.when(jnp.logical_not(end))
    def _():
        with scope("rf1"):
            for h in range(raw):
                for d in others:
                    r_add(0, 0, d, h)
                    r_copy(d, h).start()

    for k in range(2, rows - 1):
        step(k)

    @pl.when(end)
    def _():
        for k, h in first + early[:raw]:
            merge(k, h)

    @pl.when(jnp.logical_not(end))
    def _():
        with scope("rf2"):
            for h in range(raw):
                r_add(0, 0, cols, h)
                r_copy(cols, h).start()

    @pl.when(middle)
    def _():
        with scope("rn"):
            for h in range(raw):
                for d in others:
                    r_add(1, rows - 2, d, h)
                exchange(rows - 2, h)

    step(rows - 1)
    low_out[1] = x1[row].astype(F32).T.astype(BF16)

    @pl.when(middle)
    def _():
        for k, h in first:
            merge(k, h)

        with scope("rw"):
            for h in range(raw):
                r_add(1, rows - 2, cols, h)

        near = late[:raw]

        @pl.when(upper)
        def _():
            for k, h in early[:-2] + near + early[-2:]:
                merge(k, h)

        @pl.when(jnp.logical_not(upper))
        def _():
            for k, h in early[:raw] + near[:1] + early[raw:-1] + near[1:] + early[-1:]:
                merge(k, h)

    @pl.when(jnp.logical_not(middle))
    def _():
        @pl.when(jnp.logical_not(end))
        def _():
            for k, h in first:
                merge(k, h)

        @pl.when(jnp.logical_not(end))
        def _():
            for k, h in early[:raw]:
                merge(k, h)

        for k, h in early[raw:] + late[:raw]:
            merge(k, h)

        with scope("e"):

            @pl.when(end)
            def _():
                for h in range(raw, pieces):
                    for d in others:
                        e_add(d, h)
                    exchange(rows - 1, h)
                for h in range(raw, pieces):
                    e_add(cols, h)

        for k, h in late[raw:]:
            merge(k, h)

    loads[6].wait()
    loads[7].wait()
    for h in range(pieces):
        with scope("zown%d" % h):
            for slot, edge, far in ((layer, 0, last), (spare(layer), last, 0)):
                if h < raw:

                    @pl.when(layer != edge)
                    def _():
                        z_wait(slot, h)

                elif layers == 4:

                    @pl.when(layer != far)
                    def _():
                        z_wait(slot, h)

                else:
                    z_wait(slot, h)

        with scope("yown%d" % h):
            value = merged(rows - 1, h)
        with scope("fin%d" % h):
            value = value + z_in[layer, h].astype(F32) + z_in[spare(layer), h].astype(F32)
            residual = (rhs_anc[h].astype(F32) - value).astype(BF16)
            anc_out[h] = dot_t(residual, inv_anc[h])

    with scope("sent"):
        total = 2 * chips + rows - 2
        mine = goal == col
        for n, case in (
            (total, jnp.logical_not(mine)),
            (total - 2, jnp.logical_and(mine, core == 0)),
            (total - 1, jnp.logical_and(mine, core == 1)),
        ):

            @pl.when(jnp.logical_and(active, case))
            def _():
                p_sent(n)

        mate_copy(0).wait_send()
        for k in range(2, rows):

            @pl.when(row == solver(k, owner)[0])
            def _():
                x_sent(k)

        far, every = raw * cols, pieces * (cols - 1)
        kept = (pieces - raw) * (cols - 1) + every * (rows - 2) + (pieces - raw) + pieces * (rows - 3)

        @pl.when(middle)
        def _():
            sends(far + kept + raw * (cols - 1) + raw + (pieces - raw) * cols).wait_send()

        @pl.when(jnp.logical_not(middle))
        def _():
            sends(far + kept + every + pieces).wait_send()


def hand_over(low, anc, low_out, anc_out, sem):
    first = pltpu.make_async_copy(anc, anc_out, sem.at[0])
    second = pltpu.make_async_copy(low, low_out, sem.at[1])
    first.start()
    second.start()
    first.wait()
    second.wait()


def on_device(sizes, rhs_low, inv_low, blocks, targets, rhs_anc, inv_anc):
    layers, rows, cols = sizes
    levels, slots = blocks.shape[3], blocks.shape[4]
    width, cases = rhs_low.shape[3], rhs_low.shape[4]
    anc_row, narrow = rhs_anc.shape[0], rhs_anc.shape[2]
    share = cases // rows
    pieces, raw = anc_row, anc_row // 2
    chips = rows // 2
    places = 1 + pl.cdiv(rows - 2, chips)
    slots_z = 4 if layers == 4 else layers + 1
    assert levels == 2 and layers == rows and layers % 2 == 0 and layers > 3 and cols <= rows
    assert cols * narrow == share and anc_row % 2 == 0
    any_space = pl.BlockSpec(memory_space=pltpu.HBM)
    dma = pltpu.SemaphoreType.DMA
    low, anc = pl.pallas_call(
        functools.partial(kernel, sizes),
        out_shape=(
            pltpu.VMEM((levels, width, share), BF16),
            pltpu.VMEM((anc_row, narrow, width), F32),
        ),
        in_specs=[any_space] * 6,
        out_specs=(pl.BlockSpec(memory_space=pltpu.VMEM), pl.BlockSpec(memory_space=pltpu.VMEM)),
        scratch_shapes=[
            pltpu.VMEM((levels, width, cases), BF16),
            pltpu.VMEM((levels, width, width), BF16),
            pltpu.VMEM((slots, width, width), BF16),
            pltpu.VMEM((slots, width, width), BF16),
            pltpu.VMEM((anc_row, narrow, width), BF16),
            pltpu.VMEM((anc_row, width, width), BF16),
            pltpu.VMEM((cases, width), BF16),
            pltpu.VMEM((rows, share, width), BF16),
            pltpu.VMEM((rows, share, width), BF16),
            pltpu.VMEM((places, cols, share, width), BF16),
            pltpu.VMEM((cases, width), F32),
            pltpu.VMEM((cases, anc_row * width), F32),
            pltpu.VMEM((cols * rows * pieces, narrow, width), BF16),
            pltpu.VMEM((cols - 1, rows, pieces, narrow, width), BF16),
            pltpu.VMEM((rows - 1, pieces, narrow, width), BF16),
            pltpu.VMEM((slots_z, pieces, narrow, width), BF16),
            pltpu.VMEM((2, cols, raw, narrow, width), BF16),
            pltpu.VMEM((cols, pieces - raw, narrow, width), BF16),
            pltpu.SMEM((levels, slots), jnp.int32),
            dma((9,)),
            dma,
            dma((places, cols)),
            dma((rows - 1,)),
            dma((rows,)),
            dma((cols - 1, rows * pieces - raw)),
            dma((slots_z, pieces)),
            dma((2, (cols - 1) * raw + 1)),
            dma(((cols - 1) * (pieces - raw) + 1,)),
            dma,
        ],
        compiler_params=pltpu.CompilerParams(
            collective_id=0, has_side_effects=True, vmem_limit_bytes=56 * 1024 * 1024
        ),
    )(
        targets.reshape(levels, slots),
        rhs_low.reshape(levels, width, cases),
        inv_low.reshape(levels, width, width),
        blocks.reshape(levels, slots, width, width),
        rhs_anc.transpose(0, 2, 1),
        inv_anc,
    )
    low, anc = pl.pallas_call(
        hand_over,
        out_shape=(
            jax.ShapeDtypeStruct(low.shape, low.dtype),
            jax.ShapeDtypeStruct(anc.shape, anc.dtype),
        ),
        in_specs=[pl.BlockSpec(memory_space=pltpu.VMEM)] * 2,
        out_specs=(any_space, any_space),
        scratch_shapes=[dma((2,))],
        compiler_params=pltpu.CompilerParams(vmem_limit_bytes=4 * 1024 * 1024),
    )(low, anc)
    return low[None, :, None], anc.transpose(0, 2, 1)


def solution(mesh):
    sizes = tuple(mesh.shape[a] for a in ("layer", "row", "col"))
    in_specs = (
        P("layer", None, "col", None, None),
        P("layer", None, "col", None, None),
        P("layer", "row", "col", None, None, None, None),
        P("layer", "row", "col", None, None),
        P("row", None, ("layer", "col")),
        P("row", None, None),
    )
    out_specs = (P("layer", None, "col", None, "row"), P("row", None, ("layer", "col")))
    return jax.shard_map(
        functools.partial(on_device, sizes),
        mesh=mesh,
        in_specs=in_specs,
        out_specs=out_specs,
        check_vma=False,
    )
```

```python
import contextlib
import functools

import jax
import jax.numpy as jnp
from jax import lax
from jax.experimental import pallas as pl
from jax.experimental.pallas import tpu as pltpu
from jax.sharding import PartitionSpec as P

MESH = pl.DeviceIdType.MESH
F32 = jnp.float32
BF16 = jnp.bfloat16


def scope(name):
    return contextlib.nullcontext()


def dot_t(left, right):
    return lax.dot_general(left, right, (((1,), (1,)), ((), ())), preferred_element_type=F32)


def flag(condition):
    return condition.astype(jnp.int32)


def ranked(layer, layers):
    low = flag(layer < layers // 2)
    far, near = low * (layers - 1), (1 - low) * (layers - 1)
    keys = []
    for j in range(layers):
        key = -2 * layers * jnp.abs(layer - j) - j
        key = key - 1000 * layers * flag(far == j) + 1000 * layers * flag(near == j)
        keys.append(key + 5000 * layers * flag(layer == j))
    order = [0] * layers
    for j in range(layers):
        rank = 0
        for other in range(layers):
            if other != j:
                rank = rank + flag(keys[other] < keys[j])
        order = [order[k] + j * flag(rank == k) for k in range(layers)]
    return order


def kernel(
    sizes,
    targets_hbm,
    rhs_hbm,
    inv_hbm,
    blocks_hbm,
    rhs_anc_hbm,
    inv_anc_hbm,
    low_out,
    anc_out,
    rhs,
    inv,
    blocks0,
    blocks1,
    rhs_anc,
    inv_anc,
    x0,
    x1,
    part,
    part_in,
    rhs_t,
    base,
    packed,
    y_in,
    z_out,
    z_in,
    r_in,
    targets,
    load_sem,
    p_send,
    p_recv,
    x_send,
    x_recv,
    y_recv,
    z_recv,
    r_recv,
    send_sem,
):
    layers, rows, cols = sizes
    layer, row, col = (lax.axis_index(a) for a in ("layer", "row", "col"))
    slots = blocks0.shape[0]
    anc_row, narrow, width = rhs_anc.shape
    share = x1.shape[1]
    pieces = anc_row
    raw = pieces // 2
    chips = rows // 2
    last = layers - 1

    chip, core = row // 2, row % 2
    mate = row + 1 - 2 * core
    order = ranked(layer, layers)
    goal = (row + rows - 1) % rows
    active = goal < cols
    owner = (1 + col) % rows

    loads = [
        pltpu.make_async_copy(source, target, load_sem.at[n])
        for n, source, target in (
            (0, inv_hbm.at[0], inv.at[0]),
            (1, rhs_hbm.at[0], rhs.at[0]),
            (2, blocks_hbm.at[0], blocks0),
            (0, inv_hbm.at[1], inv.at[1]),
            (1, rhs_hbm.at[1], rhs.at[1]),
            (2, blocks_hbm.at[1], blocks1),
            (3, inv_anc_hbm, inv_anc),
            (0, rhs_anc_hbm, rhs_anc),
            (3, targets_hbm, targets),
        )
    ]
    for n in (0, 1):
        loads[n].start()

    barrier = pltpu.get_barrier_semaphore()

    def greet(device):
        pl.semaphore_signal(barrier, inc=1, device_id=device, device_id_type=MESH)

    for d in range(1, rows):
        greet({"row": (row + d) % rows})
    for d in range(1, cols):
        greet({"col": (col + d) % cols})
    for step in (-1, 1):

        @pl.when(jnp.logical_and(layer + step >= 0, layer + step < layers))
        def _():
            greet({"layer": layer + step})

    for cc in range(cols):

        @pl.when(col != cc)
        def _():
            greet({"row": owner, "col": cc})

    @pl.when(jnp.logical_and(active, col != goal))
    def _():
        for r in range(rows):
            greet({"row": r, "col": goal})

    met = (rows - 1) + (cols - 1) + flag(layer > 0) + flag(layer < last)
    met = met + (cols - 1) + flag(jnp.logical_and(active, col != goal)) * rows

    for n in (8, 2):
        loads[n].start()

    def spare(j):
        return (1 - j % 2) * last if layers == 4 else layers

    def at(cc, k, h):
        return (cc * rows + k) * pieces + h

    def sends(n):
        return pltpu.make_async_remote_copy(
            src_ref=packed.at[0:n],
            dst_ref=packed.at[0:n],
            send_sem=send_sem,
            recv_sem=send_sem,
            device_id={"row": mate},
            device_id_type=MESH,
        )

    def listed(level, target):
        index, found = jnp.int32(0), jnp.int32(0)
        for s in range(slots):
            hit = (targets[level, s] == target).astype(jnp.int32)
            index = index + hit * s
            found = found + hit
        return (blocks0, blocks1)[level][index], found.astype(F32)

    def span(j):
        return pl.ds(pl.multiple_of(j * share, share), share)

    def solver(k, source):
        if k < 2:
            return [2 * ((source // 2 + 1 + ch) % chips) + k for ch in range(chips)]
        return [2 * ((source // 2 + k - 2) % chips)]

    def place(k):
        return 0 if k < 2 else 1 + (k - 2) // chips

    def p_copy(k, n):
        return pltpu.make_async_remote_copy(
            src_ref=part.at[k],
            dst_ref=part_in.at[place(k), col],
            send_sem=p_send,
            recv_sem=p_recv.at[place(k), col],
            device_id={"row": solver(k, row)[n], "col": goal},
            device_id_type=MESH,
        )

    def here(k, n):
        return jnp.logical_and(goal == col, row == solver(k, row)[n])

    def part_of(k):
        block, found = listed(0, 1)
        part[k] = (dot_t(x0[span(order[k]), :], block) * found).astype(BF16)

    def part_out(k):
        for n in range(len(solver(k, row))):

            @pl.when(jnp.logical_not(here(k, n)))
            def _():
                p_copy(k, n).start()

            @pl.when(here(k, n))
            def _():
                part_in[place(k), col] = part[k]

    def lower(k):
        if share % 128 == 0:
            first = lax.dot_general(
                rhs[0, :, span(order[k])],
                inv[0],
                (((0,), (1,)), ((), ())),
                preferred_element_type=F32,
            )
            x0[span(order[k]), :] = first.astype(BF16)
        elif k == 0:
            first = jnp.dot(inv[0], rhs[0], preferred_element_type=F32)
            x0[...] = first.T.astype(BF16)

    with scope("ldx0"):
        loads[0].wait()
        loads[1].wait()
    for n in (3, 4):
        loads[n].start()
    with scope("x0"):
        lower(0)
    loads[8].wait()
    loads[2].wait()
    for n in (5, 6):
        loads[n].start()

    @pl.when(active)
    def _():
        part_of(0)

    with scope("barr"):
        pl.semaphore_wait(barrier, met)

    with scope("part"):

        @pl.when(active)
        def _():
            part_out(0)
            for k in range(1, rows):
                lower(k)
                part_of(k)
                part_out(k)

        @pl.when(jnp.logical_not(active))
        def _():
            for k in range(1, rows):
                lower(k)

    loads[3].wait()
    loads[7].start()
    loads[4].wait()
    rhs_t[...] = rhs[1].astype(F32).T

    with scope("base"):
        for a in range(anc_row):
            block, found = listed(0, a + 2)
            base[:, a * width : (a + 1) * width] = dot_t(x0[...], block) * found

    for j in range(rows):

        @pl.when(row == j)
        def _():
            low_out[0] = x0[j * share : (j + 1) * share, :].astype(F32).T.astype(BF16)

    def blank(edge, slot, h):
        @pl.when(layer == edge)
        def _():
            z_in[slot, h] = jnp.zeros_like(z_in[slot, h])

    for h in range(pieces):
        if h < raw:
            blank(0, 0, h)
        elif layers == 4:
            blank(0, spare(0), h)
        if h <= raw:
            blank(last, spare(last), h)
        elif layers == 4:
            blank(last, last, h)

    loads[5].wait()

    def mate_copy(k):
        return pltpu.make_async_remote_copy(
            src_ref=x1.at[order[k]],
            dst_ref=x1.at[order[k]],
            send_sem=x_send.at[0],
            recv_sem=x_recv.at[k],
            device_id={"row": mate},
            device_id_type=MESH,
        )

    def x_copy(k, d):
        return pltpu.make_async_remote_copy(
            src_ref=x1.at[order[k]],
            dst_ref=x1.at[order[k]],
            send_sem=x_send.at[place(k)],
            recv_sem=x_recv.at[k],
            device_id={"row": (row + d) % rows},
            device_id_type=MESH,
        )

    def p_sent(n):
        pltpu.make_async_remote_copy(
            src_ref=packed.at[0 : n * cols],
            dst_ref=packed.at[0 : n * cols],
            send_sem=p_send,
            recv_sem=p_send,
            device_id={"row": mate},
            device_id_type=MESH,
        ).wait_send()

    def x_sent(k):
        pltpu.make_async_remote_copy(
            src_ref=x1.at[0 : rows - 1],
            dst_ref=x1.at[0 : rows - 1],
            send_sem=x_send.at[place(k)],
            recv_sem=x_send.at[place(k)],
            device_id={"row": mate},
            device_id_type=MESH,
        ).wait_send()

    def solve(k):
        for cc in range(cols):

            @pl.when(jnp.logical_or(col != cc, row != owner))
            def _():
                pltpu.make_async_remote_copy(
                    src_ref=part.at[0],
                    dst_ref=part_in.at[place(k), cc],
                    send_sem=p_send,
                    recv_sem=p_recv.at[place(k), cc],
                    device_id={"row": mate},
                    device_id_type=MESH,
                ).wait_recv()

        total = part_in[place(k), 0].astype(F32)
        for cc in range(1, cols):
            total = total + part_in[place(k), cc].astype(F32)
        residual = (rhs_t[span(order[k]), :] - total).astype(BF16)
        x1[order[k]] = dot_t(residual, inv[1]).astype(BF16)

    def solve_all(k):
        @pl.when(row == solver(k, owner)[0])
        def _():
            solve(k)
            for d in range(1, rows):
                x_copy(k, d).start()

    def y_copy(d, k, h):
        cc = (col + d) % cols
        return pltpu.make_async_remote_copy(
            src_ref=packed.at[at(cc, k, h)],
            dst_ref=y_in.at[d - 1, k, h],
            send_sem=send_sem,
            recv_sem=y_recv.at[d - 1, k * pieces + h - raw],
            device_id={"col": cc},
            device_id_type=MESH,
        )

    others, whole = range(1, cols), range(1, cols + 1)
    plain = [(h, h + 1) for h in range(0, pieces, 2)]
    mixed = [(h, h + raw) for h in range(pieces - raw)] + [(h,) for h in range(pieces - raw, raw)]

    def products(k):
        @pl.when(core != k if k < 2 else row != solver(k, owner)[0])
        def _():
            mate_copy(k).wait_recv()

        j = order[k]
        for pair in plain if k else mixed:
            for a in pair:
                block, found = listed(1, a + 2)
                lanes = slice(a * width, (a + 1) * width)
                value = base[span(j), lanes] + dot_t(x1[j], block) * found
                value = value.astype(BF16)
                for cc in range(cols):
                    packed[at(cc, k, a)] = value[cc * narrow : (cc + 1) * narrow]
            for a in pair:
                sent(k, a)

    end = jnp.logical_or(layer == 0, layer == last)
    middle = jnp.logical_or(layer == layers // 2 - 1, layer == layers // 2)
    upper = layer == layers // 2
    beside = jnp.logical_or(layer == layers // 2 - 2, layer == layers // 2 + 1)
    low = layer < layers // 2
    high = jnp.logical_not(low)
    onward = layer + 2 * flag(order[0] > layer) - 1


    def sent(k, h):
        if k == 0 and h < raw:

            @pl.when(end)
            def _():
                for d in others:
                    r_copy(d, h).start()
                if h == raw - 1:
                    for n in range(raw):
                        r_copy(cols, n).start()

            if h == raw - 1:

                @pl.when(jnp.logical_and(end, low))
                def _():
                    r_copy(cols, raw).start()

        elif k == 0 and h == raw:

            @pl.when(jnp.logical_and(end, low))
            def _():
                for d in others:
                    r_copy(d, h).start()

            @pl.when(high)
            def _():
                exchange(k, h)

        elif k == rows - 2:
            if h >= raw:

                @pl.when(jnp.logical_and(middle, low) if h == raw else middle)
                def _():
                    for d in others:
                        e_copy(d, h).start()

            if h == pieces - 1:

                @pl.when(middle)
                def _():
                    for n in range(raw + 1, pieces):
                        e_copy(cols, n).start()

                @pl.when(jnp.logical_and(middle, low))
                def _():
                    e_copy(cols, raw).start()

            @pl.when(jnp.logical_not(middle))
            def _():
                exchange(k, h)

        elif k == rows - 1 and h >= raw:

            @pl.when(jnp.logical_not(jnp.logical_and(end, low) if h == raw else end))
            def _():
                exchange(k, h)

        else:
            exchange(k, h)

    def exchange(k, h):
        for d in range(1, cols):
            y_copy(d, k, h).start()

    def r_place(d, h):
        return (d - 1) * (raw + 1) + h if d < cols else (cols - 1) * (raw + 1)

    def r_copy(d, h):
        cc = (col + d) % cols
        return pltpu.make_async_remote_copy(
            src_ref=packed.at[at(cc, 0, h)],
            dst_ref=r_in.at[flag(middle), d - 1, h],
            send_sem=send_sem,
            recv_sem=r_recv.at[flag(middle), r_place(d, h)],
            device_id={"layer": onward},
            device_id_type=MESH,
        )

    def r_wait(slot, d, h, n):
        where = r_in.at[slot, d - 1, 0:n] if n else r_in.at[slot, d - 1, h]
        pltpu.make_async_remote_copy(
            src_ref=where,
            dst_ref=where,
            send_sem=send_sem,
            recv_sem=r_recv.at[slot, r_place(d, h)],
            device_id={"layer": onward},
            device_id_type=MESH,
        ).wait_recv()

    def r_add(slot, k, d, h, place=0):
        cc = (col + d) % cols
        value = packed[at(cc, k, h)].astype(F32) + r_in[slot, d - 1, h - place].astype(F32)
        packed[at(cc, k, h)] = value.astype(BF16)

    def r_others(slot, k, wider, then):
        for h in range(raw):
            for d in others:
                r_wait(slot, d, h, 0)
                r_add(slot, k, d, h)
            then(h)

        @pl.when(wider)
        def _():
            for d in others:
                r_wait(slot, d, raw, 0)
                r_add(slot, k, d, raw)
            then(raw)

    def r_own(slot, k, wider, then):
        for n, case in ((raw, jnp.logical_not(wider)), (raw + 1, wider)):

            @pl.when(case)
            def _():
                r_wait(slot, cols, 0, n)
                for h in range(n):
                    r_add(slot, k, cols, h)
                    then(h)

    def e_copy(d, h):
        cc = (col + d) % cols
        return pltpu.make_async_remote_copy(
            src_ref=packed.at[at(cc, rows - 2, h)],
            dst_ref=r_in.at[0, d - 1, h - raw],
            send_sem=send_sem,
            recv_sem=r_recv.at[0, r_place(d, h - raw)],
            device_id={"layer": order[rows - 2]},
            device_id_type=MESH,
        )

    def e_own(n):
        where = r_in.at[0, cols - 1, pieces - raw - n : pieces - raw]
        pltpu.make_async_remote_copy(
            src_ref=where,
            dst_ref=where,
            send_sem=send_sem,
            recv_sem=r_recv.at[0, r_place(cols, 0)],
            device_id={"layer": onward},
            device_id_type=MESH,
        ).wait_recv()
        for h in range(pieces - n, pieces):
            r_add(0, rows - 1, cols, h, raw)

    def e_others(h):
        for d in others:
            r_wait(0, d, h - raw, 0)
            r_add(0, rows - 1, d, h, raw)
        exchange(rows - 1, h)

    def z_copy(k, h):
        j = order[k]
        toward = layer + 2 * flag(j > layer) - 1
        if k == 0:
            toward = toward + flag(middle) * (j - toward)
        other = jnp.logical_and(j == toward, j < layer)
        if k == 0:
            other = jnp.logical_and(j == toward, jnp.logical_xor(j < layer, middle))
        slot = j + flag(other) * (spare(j) - j)
        return pltpu.make_async_remote_copy(
            src_ref=z_out.at[k, h],
            dst_ref=z_in.at[slot, h],
            send_sem=send_sem,
            recv_sem=z_recv.at[slot, h],
            device_id={"layer": toward},
            device_id_type=MESH,
        )

    def z_wait(slot, h):
        pltpu.make_async_remote_copy(
            src_ref=z_out.at[0, h],
            dst_ref=z_in.at[slot, h],
            send_sem=send_sem,
            recv_sem=z_recv.at[slot, h],
            device_id={"layer": (layer + 1) % layers},
            device_id_type=MESH,
        ).wait_recv()

    def merged(k, h):
        for d in range(1, cols):
            y_copy(d, k, h).wait_recv()
        value = packed[at(col, k, h)].astype(F32)
        for d in range(1, cols):
            value = value + y_in[d - 1, k, h].astype(F32)
        return value

    def merge(k, h):
        with scope("y%d%d" % (k, h)):
            value = merged(k, h)
        j = order[k]
        passing = jnp.logical_or(
            jnp.logical_and(j > layer, layer > 0), jnp.logical_and(j < layer, layer < last)
        )
        if k == rows - 2:
            passing = jnp.logical_and(passing, jnp.logical_not(middle))
            if h == raw:
                passing = jnp.logical_and(passing, jnp.logical_not(jnp.logical_and(beside, low)))
            elif h > raw:
                passing = jnp.logical_and(passing, jnp.logical_not(beside))

        with scope("z%d%d" % (k, h)):

            @pl.when(passing)
            def _():
                z_wait(j, h)
                z_out[k, h] = (value + z_in[j, h].astype(F32)).astype(BF16)

            @pl.when(jnp.logical_not(passing))
            def _():
                z_out[k, h] = value.astype(BF16)

        z_copy(k, h).start()

    def solve_own(k):
        @pl.when(core == k)
        def _():
            with scope("x1"):
                solve(k)
            mate_copy(k).start()

    def first():
        @pl.when(high)
        def _():
            merge(0, raw)

        for h in range(raw + 1, pieces):
            merge(0, h)

    early = [(k, h) for k in range(1, rows - 2) for h in range(pieces)]
    late = [(rows - 2, h) for h in range(pieces)]

    def step(k):
        with scope("p%d" % k):
            products(k)

    solve_own(0)
    solve_own(1)
    step(0)
    with scope("x1_2"):
        solve_all(2)
    step(1)
    with scope("x1_3"):
        for k in range(3, rows):
            solve_all(k)

    @pl.when(jnp.logical_not(end))
    def _():
        with scope("rf1"):
            r_others(0, 0, low, lambda h: [r_copy(d, h).start() for d in others])

    beyond = jnp.logical_and(end, chip != owner // 2)

    @pl.when(end)
    def _():
        first()

    @pl.when(beyond)
    def _():
        for k, h in early[:raw]:
            merge(k, h)

    for k in range(2, rows - 1):
        step(k)

    @pl.when(jnp.logical_and(end, jnp.logical_not(beyond)))
    def _():
        for k, h in early[:raw]:
            merge(k, h)

    @pl.when(jnp.logical_not(end))
    def _():
        with scope("rf2"):
            r_own(0, 0, low, lambda h: r_copy(cols, h).start())

    @pl.when(middle)
    def _():
        with scope("rn"):
            r_others(1, rows - 2, high, lambda h: exchange(rows - 2, h))

    step(rows - 1)
    low_out[1] = x1[row].astype(F32).T.astype(BF16)

    @pl.when(middle)
    def _():
        first()

        @pl.when(upper)
        def _():
            for k, h in early:
                merge(k, h)

        @pl.when(jnp.logical_not(upper))
        def _():
            for k, h in early[:raw]:
                merge(k, h)

        with scope("rw"):
            r_own(1, rows - 2, high, lambda h: None)

        for k, h in late[:raw]:
            merge(k, h)

        @pl.when(upper)
        def _():
            merge(rows - 2, raw)

        @pl.when(jnp.logical_not(upper))
        def _():
            for k, h in early[raw:]:
                merge(k, h)

    @pl.when(jnp.logical_not(middle))
    def _():
        @pl.when(jnp.logical_not(end))
        def _():
            first()

        @pl.when(jnp.logical_not(end))
        def _():
            for k, h in early[:raw]:
                merge(k, h)

        for k, h in early[raw:] + late[:raw]:
            merge(k, h)

        with scope("e"):

            @pl.when(jnp.logical_and(end, low))
            def _():
                e_others(raw)

            @pl.when(end)
            def _():
                for h in range(raw + 1, pieces):
                    e_others(h)

        for k, h in late[raw:]:
            merge(k, h)

        with scope("ew"):

            @pl.when(jnp.logical_and(end, low))
            def _():
                e_own(pieces - raw)

            @pl.when(jnp.logical_and(end, high))
            def _():
                e_own(pieces - raw - 1)

    loads[6].wait()
    loads[7].wait()
    for h in range(pieces):
        with scope("zown%d" % h):
            below, above = layer >= 0, layer >= 0
            if h < raw:
                below = layer != 0
            elif layers == 4:
                above = layer != 0
            if h <= raw:
                above = jnp.logical_and(above, layer != last)
            elif layers == 4:
                below = jnp.logical_and(below, layer != last)
            for slot, case in ((layer, below), (spare(layer), above)):

                @pl.when(case)
                def _():
                    z_wait(slot, h)

        with scope("yown%d" % h):
            value = merged(rows - 1, h)
        with scope("fin%d" % h):
            value = value + z_in[layer, h].astype(F32) + z_in[spare(layer), h].astype(F32)
            residual = (rhs_anc[h].astype(F32) - value).astype(BF16)
            anc_out[h] = dot_t(residual, inv_anc[h])

    with scope("sent"):
        total = 2 * chips + rows - 2
        mine = goal == col
        for n, case in (
            (total, jnp.logical_not(mine)),
            (total - 2, jnp.logical_and(mine, core == 0)),
            (total - 1, jnp.logical_and(mine, core == 1)),
        ):

            @pl.when(jnp.logical_and(active, case))
            def _():
                p_sent(n)

        mate_copy(0).wait_send()
        for k in range(2, rows):

            @pl.when(row == solver(k, owner)[0])
            def _():
                x_sent(k)

        every = pieces * (cols - 1)
        for side, out, back in ((low, raw + 1, raw), (high, raw, raw + 1)):
            kept = out * cols + (pieces - out) * cols + every * (rows - 2) + pieces * (rows - 3)
            near = back * cols + (pieces - back) * cols

            @pl.when(jnp.logical_and(side, middle))
            def _():
                sends(kept + near).wait_send()

            @pl.when(jnp.logical_and(side, jnp.logical_not(middle)))
            def _():
                sends(kept + every + pieces).wait_send()


def hand_over(low, anc, low_out, anc_out, sem):
    first = pltpu.make_async_copy(anc, anc_out, sem.at[0])
    second = pltpu.make_async_copy(low, low_out, sem.at[1])
    first.start()
    second.start()
    first.wait()
    second.wait()


def on_device(sizes, rhs_low, inv_low, blocks, targets, rhs_anc, inv_anc):
    layers, rows, cols = sizes
    levels, slots = blocks.shape[3], blocks.shape[4]
    width, cases = rhs_low.shape[3], rhs_low.shape[4]
    anc_row, narrow = rhs_anc.shape[0], rhs_anc.shape[2]
    share = cases // rows
    pieces, raw = anc_row, anc_row // 2
    chips = rows // 2
    places = 1 + pl.cdiv(rows - 2, chips)
    slots_z = 4 if layers == 4 else layers + 1
    assert levels == 2 and layers == rows and layers % 2 == 0 and layers > 3 and cols <= rows
    assert cols * narrow == share and anc_row % 2 == 0
    any_space = pl.BlockSpec(memory_space=pltpu.HBM)
    dma = pltpu.SemaphoreType.DMA
    low, anc = pl.pallas_call(
        functools.partial(kernel, sizes),
        out_shape=(
            pltpu.VMEM((levels, width, share), BF16),
            pltpu.VMEM((anc_row, narrow, width), F32),
        ),
        in_specs=[any_space] * 6,
        out_specs=(pl.BlockSpec(memory_space=pltpu.VMEM), pl.BlockSpec(memory_space=pltpu.VMEM)),
        scratch_shapes=[
            pltpu.VMEM((levels, width, cases), BF16),
            pltpu.VMEM((levels, width, width), BF16),
            pltpu.VMEM((slots, width, width), BF16),
            pltpu.VMEM((slots, width, width), BF16),
            pltpu.VMEM((anc_row, narrow, width), BF16),
            pltpu.VMEM((anc_row, width, width), BF16),
            pltpu.VMEM((cases, width), BF16),
            pltpu.VMEM((rows, share, width), BF16),
            pltpu.VMEM((rows, share, width), BF16),
            pltpu.VMEM((places, cols, share, width), BF16),
            pltpu.VMEM((cases, width), F32),
            pltpu.VMEM((cases, anc_row * width), F32),
            pltpu.VMEM((cols * rows * pieces, narrow, width), BF16),
            pltpu.VMEM((cols - 1, rows, pieces, narrow, width), BF16),
            pltpu.VMEM((rows - 1, pieces, narrow, width), BF16),
            pltpu.VMEM((slots_z, pieces, narrow, width), BF16),
            pltpu.VMEM((2, cols, raw + 1, narrow, width), BF16),
            pltpu.SMEM((levels, slots), jnp.int32),
            dma((4,)),
            dma,
            dma((places, cols)),
            dma((places,)),
            dma((rows,)),
            dma((cols - 1, rows * pieces - raw)),
            dma((slots_z, pieces)),
            dma((2, (cols - 1) * (raw + 1) + 1)),
            dma,
        ],
        compiler_params=pltpu.CompilerParams(
            collective_id=0, has_side_effects=True, vmem_limit_bytes=56 * 1024 * 1024
        ),
    )(
        targets.reshape(levels, slots),
        rhs_low.reshape(levels, width, cases),
        inv_low.reshape(levels, width, width),
        blocks.reshape(levels, slots, width, width),
        rhs_anc.transpose(0, 2, 1),
        inv_anc,
    )
    low, anc = pl.pallas_call(
        hand_over,
        out_shape=(
            jax.ShapeDtypeStruct(low.shape, low.dtype),
            jax.ShapeDtypeStruct(anc.shape, anc.dtype),
        ),
        in_specs=[pl.BlockSpec(memory_space=pltpu.VMEM)] * 2,
        out_specs=(any_space, any_space),
        scratch_shapes=[dma((2,))],
        compiler_params=pltpu.CompilerParams(vmem_limit_bytes=4 * 1024 * 1024),
    )(low, anc)
    return low[None, :, None], anc.transpose(0, 2, 1)


def solution(mesh):
    sizes = tuple(mesh.shape[a] for a in ("layer", "row", "col"))
    in_specs = (
        P("layer", None, "col", None, None),
        P("layer", None, "col", None, None),
        P("layer", "row", "col", None, None, None, None),
        P("layer", "row", "col", None, None),
        P("row", None, ("layer", "col")),
        P("row", None, None),
    )
    out_specs = (P("layer", None, "col", None, "row"), P("row", None, ("layer", "col")))
    return jax.shard_map(
        functools.partial(on_device, sizes),
        mesh=mesh,
        in_specs=in_specs,
        out_specs=out_specs,
        check_vma=False,
    )
```

```python
import contextlib
import functools

import jax
import jax.numpy as jnp
from jax import lax
from jax.experimental import pallas as pl
from jax.experimental.pallas import tpu as pltpu
from jax.sharding import PartitionSpec as P

MESH = pl.DeviceIdType.MESH
F32 = jnp.float32
BF16 = jnp.bfloat16


def scope(name):
    return contextlib.nullcontext()


def dot_t(left, right):
    return lax.dot_general(left, right, (((1,), (1,)), ((), ())), preferred_element_type=F32)


def flag(condition):
    return condition.astype(jnp.int32)


def ranked(layer, layers):
    low = flag(layer < layers // 2)
    far, near = low * (layers - 1), (1 - low) * (layers - 1)
    keys = []
    for j in range(layers):
        key = -2 * layers * jnp.abs(layer - j) - j
        key = key - 1000 * layers * flag(far == j) + 1000 * layers * flag(near == j)
        keys.append(key + 5000 * layers * flag(layer == j))
    order = [0] * layers
    for j in range(layers):
        rank = 0
        for other in range(layers):
            if other != j:
                rank = rank + flag(keys[other] < keys[j])
        order = [order[k] + j * flag(rank == k) for k in range(layers)]
    return order


def kernel(
    sizes,
    targets_hbm,
    rhs_hbm,
    inv_hbm,
    blocks_hbm,
    rhs_anc_hbm,
    inv_anc_hbm,
    low_out,
    anc_out,
    rhs,
    inv,
    blocks0,
    blocks1,
    rhs_anc,
    inv_anc,
    x0,
    x1,
    part,
    part_in,
    rhs_t,
    base,
    packed,
    y_in,
    z_out,
    z_in,
    r_in,
    targets,
    load_sem,
    p_send,
    p_recv,
    x_send,
    x_recv,
    y_recv,
    z_recv,
    r_recv,
    send_sem,
):
    layers, rows, cols = sizes
    layer, row, col = (lax.axis_index(a) for a in ("layer", "row", "col"))
    slots = blocks0.shape[0]
    anc_row, narrow, width = rhs_anc.shape
    share = x1.shape[1]
    pieces = anc_row
    raw = pieces // 2
    chips = rows // 2
    last = layers - 1

    chip, core = row // 2, row % 2
    mate = row + 1 - 2 * core
    goal = (row + rows - 1) % rows
    active = goal < cols
    owner = (1 + col) % rows

    loads = [
        pltpu.make_async_copy(source, target, load_sem.at[n])
        for n, source, target in (
            (0, inv_hbm.at[0], inv.at[0]),
            (1, rhs_hbm.at[0], rhs.at[0]),
            (2, blocks_hbm.at[0], blocks0),
            (0, inv_hbm.at[1], inv.at[1]),
            (1, rhs_hbm.at[1], rhs.at[1]),
            (2, blocks_hbm.at[1], blocks1),
            (3, inv_anc_hbm, inv_anc),
            (0, rhs_anc_hbm, rhs_anc),
            (3, targets_hbm, targets),
        )
    ]
    for n in (0, 1):
        loads[n].start()

    barrier = pltpu.get_barrier_semaphore()

    def greet(device):
        pl.semaphore_signal(barrier, inc=1, device_id=device, device_id_type=MESH)

    for d in range(1, rows):
        greet({"row": (row + d) % rows})
    for d in range(1, cols):
        greet({"col": (col + d) % cols})
    for step in (-1, 1):

        @pl.when(jnp.logical_and(layer + step >= 0, layer + step < layers))
        def _():
            greet({"layer": layer + step})

    for cc in range(cols):

        @pl.when(col != cc)
        def _():
            greet({"row": owner, "col": cc})

    @pl.when(jnp.logical_and(active, col != goal))
    def _():
        for r in range(rows):
            greet({"row": r, "col": goal})

    met = (rows - 1) + (cols - 1) + flag(layer > 0) + flag(layer < last)
    met = met + (cols - 1) + flag(jnp.logical_and(active, col != goal)) * rows

    for n in (8, 2):
        loads[n].start()

    order = ranked(layer, layers)

    def spare(j):
        return (1 - j % 2) * last if layers == 4 else layers

    def at(cc, k, h):
        return (cc * rows + k) * pieces + h

    def sends(n):
        return pltpu.make_async_remote_copy(
            src_ref=packed.at[0:n],
            dst_ref=packed.at[0:n],
            send_sem=send_sem,
            recv_sem=send_sem,
            device_id={"row": mate},
            device_id_type=MESH,
        )

    def listed(level, target):
        index, found = jnp.int32(0), jnp.int32(0)
        for s in range(slots):
            hit = (targets[level, s] == target).astype(jnp.int32)
            index = index + hit * s
            found = found + hit
        return (blocks0, blocks1)[level][index], found.astype(F32)

    def span(j):
        return pl.ds(pl.multiple_of(j * share, share), share)

    def solver(k, source):
        if k < 2:
            return [2 * ((source // 2 + 1 + ch) % chips) + k for ch in range(chips)]
        return [2 * ((source // 2 + k - 2) % chips)]

    def place(k):
        return 0 if k < 2 else 1 + (k - 2) // chips

    def p_copy(k, n):
        return pltpu.make_async_remote_copy(
            src_ref=part.at[k],
            dst_ref=part_in.at[place(k), col],
            send_sem=p_send,
            recv_sem=p_recv.at[place(k), col],
            device_id={"row": solver(k, row)[n], "col": goal},
            device_id_type=MESH,
        )

    def here(k, n):
        return jnp.logical_and(goal == col, row == solver(k, row)[n])

    def part_of(k):
        block, found = listed(0, 1)
        part[k] = (dot_t(x0[span(order[k]), :], block) * found).astype(BF16)

    def part_out(k):
        for n in range(len(solver(k, row))):

            @pl.when(jnp.logical_not(here(k, n)))
            def _():
                p_copy(k, n).start()

            @pl.when(here(k, n))
            def _():
                part_in[place(k), col] = part[k]

    def lower(k):
        if share % 128 == 0:
            first = lax.dot_general(
                rhs[0, :, span(order[k])],
                inv[0],
                (((0,), (1,)), ((), ())),
                preferred_element_type=F32,
            )
            x0[span(order[k]), :] = first.astype(BF16)
        elif k == 0:
            first = jnp.dot(inv[0], rhs[0], preferred_element_type=F32)
            x0[...] = first.T.astype(BF16)

    with scope("ldx0"):
        loads[0].wait()
        loads[1].wait()
    for n in (3, 4):
        loads[n].start()
    with scope("x0"):
        lower(0)
    loads[8].wait()
    loads[2].wait()
    for n in (5, 6):
        loads[n].start()

    @pl.when(active)
    def _():
        part_of(0)

    with scope("barr"):
        pl.semaphore_wait(barrier, met)

    with scope("part"):

        @pl.when(active)
        def _():
            part_out(0)
            for k in range(1, rows):
                lower(k)
                part_of(k)
                part_out(k)

        @pl.when(jnp.logical_not(active))
        def _():
            for k in range(1, rows):
                lower(k)

    loads[3].wait()
    loads[7].start()
    loads[4].wait()
    rhs_t[...] = rhs[1].astype(F32).T

    with scope("base"):
        for a in range(anc_row):
            block, found = listed(0, a + 2)
            base[:, a * width : (a + 1) * width] = dot_t(x0[...], block) * found

    for j in range(rows):

        @pl.when(row == j)
        def _():
            low_out[0] = x0[j * share : (j + 1) * share, :].astype(F32).T.astype(BF16)

    def blank(edge, slot, h):
        @pl.when(layer == edge)
        def _():
            z_in[slot, h] = jnp.zeros_like(z_in[slot, h])

    for h in range(pieces):
        if h < raw:
            blank(0, 0, h)
        elif layers == 4:
            blank(0, spare(0), h)
        if h <= raw:
            blank(last, spare(last), h)
        elif layers == 4:
            blank(last, last, h)

    loads[5].wait()

    def mate_copy(k):
        return pltpu.make_async_remote_copy(
            src_ref=x1.at[order[k]],
            dst_ref=x1.at[order[k]],
            send_sem=x_send.at[0],
            recv_sem=x_recv.at[k],
            device_id={"row": mate},
            device_id_type=MESH,
        )

    def x_copy(k, d):
        return pltpu.make_async_remote_copy(
            src_ref=x1.at[order[k]],
            dst_ref=x1.at[order[k]],
            send_sem=x_send.at[place(k)],
            recv_sem=x_recv.at[k],
            device_id={"row": (row + d) % rows},
            device_id_type=MESH,
        )

    def p_sent(n):
        pltpu.make_async_remote_copy(
            src_ref=packed.at[0 : n * cols],
            dst_ref=packed.at[0 : n * cols],
            send_sem=p_send,
            recv_sem=p_send,
            device_id={"row": mate},
            device_id_type=MESH,
        ).wait_send()

    def x_sent(k):
        pltpu.make_async_remote_copy(
            src_ref=x1.at[0 : rows - 1],
            dst_ref=x1.at[0 : rows - 1],
            send_sem=x_send.at[place(k)],
            recv_sem=x_send.at[place(k)],
            device_id={"row": mate},
            device_id_type=MESH,
        ).wait_send()

    def solve(k):
        for cc in range(cols):

            @pl.when(jnp.logical_or(col != cc, row != owner))
            def _():
                pltpu.make_async_remote_copy(
                    src_ref=part.at[0],
                    dst_ref=part_in.at[place(k), cc],
                    send_sem=p_send,
                    recv_sem=p_recv.at[place(k), cc],
                    device_id={"row": mate},
                    device_id_type=MESH,
                ).wait_recv()

        total = part_in[place(k), 0].astype(F32)
        for cc in range(1, cols):
            total = total + part_in[place(k), cc].astype(F32)
        residual = (rhs_t[span(order[k]), :] - total).astype(BF16)
        x1[order[k]] = dot_t(residual, inv[1]).astype(BF16)

    def solve_all(k):
        @pl.when(row == solver(k, owner)[0])
        def _():
            solve(k)
            for d in range(1, rows):
                x_copy(k, d).start()

    def y_copy(d, k, h):
        cc = (col + d) % cols
        return pltpu.make_async_remote_copy(
            src_ref=packed.at[at(cc, k, h)],
            dst_ref=y_in.at[d - 1, k, h],
            send_sem=send_sem,
            recv_sem=y_recv.at[d - 1, k * pieces + h - raw],
            device_id={"col": cc},
            device_id_type=MESH,
        )

    others, whole = range(1, cols), range(1, cols + 1)
    plain = [(h, h + 1) for h in range(0, pieces, 2)]
    mixed = [(h, h + raw) for h in range(pieces - raw)] + [(h,) for h in range(pieces - raw, raw)]

    def products(k):
        @pl.when(core != k if k < 2 else row != solver(k, owner)[0])
        def _():
            mate_copy(k).wait_recv()

        j = order[k]
        for pair in plain if k else mixed:
            for a in pair:
                block, found = listed(1, a + 2)
                lanes = slice(a * width, (a + 1) * width)
                value = base[span(j), lanes] + dot_t(x1[j], block) * found
                value = value.astype(BF16)
                for cc in range(cols):
                    packed[at(cc, k, a)] = value[cc * narrow : (cc + 1) * narrow]
            for a in pair:
                sent(k, a)

    end = jnp.logical_or(layer == 0, layer == last)
    middle = jnp.logical_or(layer == layers // 2 - 1, layer == layers // 2)
    upper = layer == layers // 2
    beside = jnp.logical_or(layer == layers // 2 - 2, layer == layers // 2 + 1)
    low = layer < layers // 2
    high = jnp.logical_not(low)
    onward = layer + 2 * flag(order[0] > layer) - 1


    def sent(k, h):
        if k == 0 and h < raw:

            @pl.when(end)
            def _():
                for d in others:
                    r_copy(d, h).start()
                if h == raw - 1:
                    for n in range(raw):
                        r_copy(cols, n).start()

            if h == raw - 1:

                @pl.when(jnp.logical_and(end, low))
                def _():
                    r_copy(cols, raw).start()

        elif k == 0 and h == raw:

            @pl.when(jnp.logical_and(end, low))
            def _():
                for d in others:
                    r_copy(d, h).start()

            @pl.when(high)
            def _():
                exchange(k, h)

        elif k == rows - 2:
            if h >= raw:

                @pl.when(jnp.logical_and(middle, low) if h == raw else middle)
                def _():
                    for d in others:
                        e_copy(d, h).start()

            if h == pieces - 1:

                @pl.when(middle)
                def _():
                    for n in range(raw + 1, pieces):
                        e_copy(cols, n).start()

                @pl.when(jnp.logical_and(middle, low))
                def _():
                    e_copy(cols, raw).start()

            @pl.when(jnp.logical_not(middle))
            def _():
                exchange(k, h)

        elif k == rows - 1 and h >= raw:

            @pl.when(jnp.logical_not(jnp.logical_and(end, low) if h == raw else end))
            def _():
                exchange(k, h)

        else:
            exchange(k, h)

    def exchange(k, h):
        for d in range(1, cols):
            y_copy(d, k, h).start()

    def r_place(d, h):
        return (d - 1) * (raw + 1) + h if d < cols else (cols - 1) * (raw + 1)

    def r_copy(d, h):
        cc = (col + d) % cols
        return pltpu.make_async_remote_copy(
            src_ref=packed.at[at(cc, 0, h)],
            dst_ref=r_in.at[flag(middle), d - 1, h],
            send_sem=send_sem,
            recv_sem=r_recv.at[flag(middle), r_place(d, h)],
            device_id={"layer": onward},
            device_id_type=MESH,
        )

    def r_wait(slot, d, h, n):
        where = r_in.at[slot, d - 1, 0:n] if n else r_in.at[slot, d - 1, h]
        pltpu.make_async_remote_copy(
            src_ref=where,
            dst_ref=where,
            send_sem=send_sem,
            recv_sem=r_recv.at[slot, r_place(d, h)],
            device_id={"layer": onward},
            device_id_type=MESH,
        ).wait_recv()

    def r_add(slot, k, d, h, place=0):
        cc = (col + d) % cols
        value = packed[at(cc, k, h)].astype(F32) + r_in[slot, d - 1, h - place].astype(F32)
        packed[at(cc, k, h)] = value.astype(BF16)

    def r_others(slot, k, wider, then):
        for h in range(raw):
            for d in others:
                r_wait(slot, d, h, 0)
                r_add(slot, k, d, h)
            then(h)

        @pl.when(wider)
        def _():
            for d in others:
                r_wait(slot, d, raw, 0)
                r_add(slot, k, d, raw)
            then(raw)

    def r_own(slot, k, wider, then):
        for n, case in ((raw, jnp.logical_not(wider)), (raw + 1, wider)):

            @pl.when(case)
            def _():
                r_wait(slot, cols, 0, n)
                for h in range(n):
                    r_add(slot, k, cols, h)
                    then(h)

    def e_copy(d, h):
        cc = (col + d) % cols
        return pltpu.make_async_remote_copy(
            src_ref=packed.at[at(cc, rows - 2, h)],
            dst_ref=r_in.at[0, d - 1, h - raw],
            send_sem=send_sem,
            recv_sem=r_recv.at[0, r_place(d, h - raw)],
            device_id={"layer": order[rows - 2]},
            device_id_type=MESH,
        )

    def e_own(n):
        where = r_in.at[0, cols - 1, pieces - raw - n : pieces - raw]
        pltpu.make_async_remote_copy(
            src_ref=where,
            dst_ref=where,
            send_sem=send_sem,
            recv_sem=r_recv.at[0, r_place(cols, 0)],
            device_id={"layer": onward},
            device_id_type=MESH,
        ).wait_recv()
        for h in range(pieces - n, pieces):
            r_add(0, rows - 1, cols, h, raw)

    def e_others(h):
        for d in others:
            r_wait(0, d, h - raw, 0)
            r_add(0, rows - 1, d, h, raw)
        exchange(rows - 1, h)

    def z_copy(k, h):
        j = order[k]
        toward = layer + 2 * flag(j > layer) - 1
        if k == 0:
            toward = toward + flag(middle) * (j - toward)
        other = jnp.logical_and(j == toward, j < layer)
        if k == 0:
            other = jnp.logical_and(j == toward, jnp.logical_xor(j < layer, middle))
        slot = j + flag(other) * (spare(j) - j)
        return pltpu.make_async_remote_copy(
            src_ref=z_out.at[k, h],
            dst_ref=z_in.at[slot, h],
            send_sem=send_sem,
            recv_sem=z_recv.at[slot, h],
            device_id={"layer": toward},
            device_id_type=MESH,
        )

    def z_wait(slot, h):
        pltpu.make_async_remote_copy(
            src_ref=z_out.at[0, h],
            dst_ref=z_in.at[slot, h],
            send_sem=send_sem,
            recv_sem=z_recv.at[slot, h],
            device_id={"layer": (layer + 1) % layers},
            device_id_type=MESH,
        ).wait_recv()

    def merged(k, h):
        for d in range(1, cols):
            y_copy(d, k, h).wait_recv()
        value = packed[at(col, k, h)].astype(F32)
        for d in range(1, cols):
            value = value + y_in[d - 1, k, h].astype(F32)
        return value

    def merge(k, h):
        with scope("y%d%d" % (k, h)):
            value = merged(k, h)
        j = order[k]
        passing = jnp.logical_or(
            jnp.logical_and(j > layer, layer > 0), jnp.logical_and(j < layer, layer < last)
        )
        if k == rows - 2:
            passing = jnp.logical_and(passing, jnp.logical_not(middle))
            if h == raw:
                passing = jnp.logical_and(passing, jnp.logical_not(jnp.logical_and(beside, low)))
            elif h > raw:
                passing = jnp.logical_and(passing, jnp.logical_not(beside))

        with scope("z%d%d" % (k, h)):

            @pl.when(passing)
            def _():
                z_wait(j, h)
                z_out[k, h] = (value + z_in[j, h].astype(F32)).astype(BF16)

            @pl.when(jnp.logical_not(passing))
            def _():
                z_out[k, h] = value.astype(BF16)

        z_copy(k, h).start()

    def solve_own(k):
        @pl.when(core == k)
        def _():
            with scope("x1"):
                solve(k)
            mate_copy(k).start()

    def first():
        @pl.when(high)
        def _():
            merge(0, raw)

        for h in range(raw + 1, pieces):
            merge(0, h)

    early = [(k, h) for k in range(1, rows - 2) for h in range(pieces)]
    late = [(rows - 2, h) for h in range(pieces)]

    def step(k):
        with scope("p%d" % k):
            products(k)

    solve_own(0)
    solve_own(1)
    step(0)
    with scope("x1_2"):
        solve_all(2)
    step(1)
    with scope("x1_3"):
        for k in range(3, rows):
            solve_all(k)

    @pl.when(jnp.logical_not(end))
    def _():
        with scope("rf1"):
            r_others(0, 0, low, lambda h: [r_copy(d, h).start() for d in others])

    beyond = jnp.logical_and(end, chip != owner // 2)

    @pl.when(end)
    def _():
        first()

    @pl.when(beyond)
    def _():
        for k, h in early[:raw]:
            merge(k, h)

    for k in range(2, rows - 1):
        step(k)

    @pl.when(jnp.logical_and(end, jnp.logical_not(beyond)))
    def _():
        for k, h in early[:raw]:
            merge(k, h)

    @pl.when(jnp.logical_not(end))
    def _():
        with scope("rf2"):
            r_own(0, 0, low, lambda h: r_copy(cols, h).start())

    @pl.when(middle)
    def _():
        with scope("rn"):
            r_others(1, rows - 2, high, lambda h: exchange(rows - 2, h))

    step(rows - 1)
    low_out[1] = x1[row].astype(F32).T.astype(BF16)

    @pl.when(middle)
    def _():
        first()

        for k, h in early[:raw]:
            merge(k, h)

        with scope("rw"):
            r_own(1, rows - 2, high, lambda h: None)

        for k, h in late[:raw]:
            merge(k, h)

        @pl.when(upper)
        def _():
            merge(rows - 2, raw)

        for k, h in early[raw:]:
            merge(k, h)

    @pl.when(jnp.logical_not(middle))
    def _():
        @pl.when(jnp.logical_not(end))
        def _():
            first()

        @pl.when(jnp.logical_not(end))
        def _():
            for k, h in early[:raw]:
                merge(k, h)

        for k, h in early[raw:] + late[:raw]:
            merge(k, h)

        with scope("e"):

            @pl.when(jnp.logical_and(end, low))
            def _():
                e_others(raw)

            @pl.when(end)
            def _():
                for h in range(raw + 1, pieces):
                    e_others(h)

        for k, h in late[raw:]:
            merge(k, h)

        with scope("ew"):

            @pl.when(jnp.logical_and(end, low))
            def _():
                e_own(pieces - raw)

            @pl.when(jnp.logical_and(end, high))
            def _():
                e_own(pieces - raw - 1)

    loads[6].wait()
    loads[7].wait()
    for h in range(pieces):
        with scope("zown%d" % h):
            below, above = layer >= 0, layer >= 0
            if h < raw:
                below = layer != 0
            elif layers == 4:
                above = layer != 0
            if h <= raw:
                above = jnp.logical_and(above, layer != last)
            elif layers == 4:
                below = jnp.logical_and(below, layer != last)
            for slot, case in ((layer, below), (spare(layer), above)):

                @pl.when(case)
                def _():
                    z_wait(slot, h)

        with scope("yown%d" % h):
            value = merged(rows - 1, h)
        with scope("fin%d" % h):
            value = value + z_in[layer, h].astype(F32) + z_in[spare(layer), h].astype(F32)
            residual = (rhs_anc[h].astype(F32) - value).astype(BF16)
            anc_out[h] = dot_t(residual, inv_anc[h])

    with scope("sent"):
        total = 2 * chips + rows - 2
        mine = goal == col
        for n, case in (
            (total, jnp.logical_not(mine)),
            (total - 2, jnp.logical_and(mine, core == 0)),
            (total - 1, jnp.logical_and(mine, core == 1)),
        ):

            @pl.when(jnp.logical_and(active, case))
            def _():
                p_sent(n)

        mate_copy(0).wait_send()
        for k in range(2, rows):

            @pl.when(row == solver(k, owner)[0])
            def _():
                x_sent(k)

        every = pieces * (cols - 1)
        for side, out, back in ((low, raw + 1, raw), (high, raw, raw + 1)):
            kept = out * cols + (pieces - out) * cols + every * (rows - 2) + pieces * (rows - 3)
            near = back * cols + (pieces - back) * cols

            @pl.when(jnp.logical_and(side, middle))
            def _():
                sends(kept + near).wait_send()

            @pl.when(jnp.logical_and(side, jnp.logical_not(middle)))
            def _():
                sends(kept + every + pieces).wait_send()


def hand_over(low, anc, low_out, anc_out, sem):
    first = pltpu.make_async_copy(anc, anc_out, sem.at[0])
    second = pltpu.make_async_copy(low, low_out, sem.at[1])
    first.start()
    second.start()
    first.wait()
    second.wait()


def on_device(sizes, rhs_low, inv_low, blocks, targets, rhs_anc, inv_anc):
    layers, rows, cols = sizes
    levels, slots = blocks.shape[3], blocks.shape[4]
    width, cases = rhs_low.shape[3], rhs_low.shape[4]
    anc_row, narrow = rhs_anc.shape[0], rhs_anc.shape[2]
    share = cases // rows
    pieces, raw = anc_row, anc_row // 2
    chips = rows // 2
    places = 1 + pl.cdiv(rows - 2, chips)
    slots_z = 4 if layers == 4 else layers + 1
    assert levels == 2 and layers == rows and layers % 2 == 0 and layers > 3 and cols <= rows
    assert cols * narrow == share and anc_row % 2 == 0
    any_space = pl.BlockSpec(memory_space=pltpu.HBM)
    dma = pltpu.SemaphoreType.DMA
    low, anc = pl.pallas_call(
        functools.partial(kernel, sizes),
        out_shape=(
            pltpu.VMEM((levels, width, share), BF16),
            pltpu.VMEM((anc_row, narrow, width), F32),
        ),
        in_specs=[any_space] * 6,
        out_specs=(pl.BlockSpec(memory_space=pltpu.VMEM), pl.BlockSpec(memory_space=pltpu.VMEM)),
        scratch_shapes=[
            pltpu.VMEM((levels, width, cases), BF16),
            pltpu.VMEM((levels, width, width), BF16),
            pltpu.VMEM((slots, width, width), BF16),
            pltpu.VMEM((slots, width, width), BF16),
            pltpu.VMEM((anc_row, narrow, width), BF16),
            pltpu.VMEM((anc_row, width, width), BF16),
            pltpu.VMEM((cases, width), BF16),
            pltpu.VMEM((rows, share, width), BF16),
            pltpu.VMEM((rows, share, width), BF16),
            pltpu.VMEM((places, cols, share, width), BF16),
            pltpu.VMEM((cases, width), F32),
            pltpu.VMEM((cases, anc_row * width), F32),
            pltpu.VMEM((cols * rows * pieces, narrow, width), BF16),
            pltpu.VMEM((cols - 1, rows, pieces, narrow, width), BF16),
            pltpu.VMEM((rows - 1, pieces, narrow, width), BF16),
            pltpu.VMEM((slots_z, pieces, narrow, width), BF16),
            pltpu.VMEM((2, cols, raw + 1, narrow, width), BF16),
            pltpu.SMEM((levels, slots), jnp.int32),
            dma((4,)),
            dma,
            dma((places, cols)),
            dma((places,)),
            dma((rows,)),
            dma((cols - 1, rows * pieces - raw)),
            dma((slots_z, pieces)),
            dma((2, (cols - 1) * (raw + 1) + 1)),
            dma,
        ],
        compiler_params=pltpu.CompilerParams(
            collective_id=0, has_side_effects=True, vmem_limit_bytes=56 * 1024 * 1024
        ),
    )(
        targets.reshape(levels, slots),
        rhs_low.reshape(levels, width, cases),
        inv_low.reshape(levels, width, width),
        blocks.reshape(levels, slots, width, width),
        rhs_anc.transpose(0, 2, 1),
        inv_anc,
    )
    low, anc = pl.pallas_call(
        hand_over,
        out_shape=(
            jax.ShapeDtypeStruct(low.shape, low.dtype),
            jax.ShapeDtypeStruct(anc.shape, anc.dtype),
        ),
        in_specs=[pl.BlockSpec(memory_space=pltpu.VMEM)] * 2,
        out_specs=(any_space, any_space),
        scratch_shapes=[dma((2,))],
        compiler_params=pltpu.CompilerParams(vmem_limit_bytes=4 * 1024 * 1024),
    )(low, anc)
    return low[None, :, None], anc.transpose(0, 2, 1)


def solution(mesh):
    sizes = tuple(mesh.shape[a] for a in ("layer", "row", "col"))
    in_specs = (
        P("layer", None, "col", None, None),
        P("layer", None, "col", None, None),
        P("layer", "row", "col", None, None, None, None),
        P("layer", "row", "col", None, None),
        P("row", None, ("layer", "col")),
        P("row", None, None),
    )
    out_specs = (P("layer", None, "col", None, "row"), P("row", None, ("layer", "col")))
    return jax.shard_map(
        functools.partial(on_device, sizes),
        mesh=mesh,
        in_specs=in_specs,
        out_specs=out_specs,
        check_vma=False,
    )
```

```python
import contextlib
import functools

import jax
import jax.numpy as jnp
from jax import lax
from jax.experimental import pallas as pl
from jax.experimental.pallas import tpu as pltpu
from jax.sharding import PartitionSpec as P

MESH = pl.DeviceIdType.MESH
F32 = jnp.float32
BF16 = jnp.bfloat16


def scope(name):
    return contextlib.nullcontext()


def dot_t(left, right):
    return lax.dot_general(left, right, (((1,), (1,)), ((), ())), preferred_element_type=F32)


def flag(condition):
    return condition.astype(jnp.int32)


def ranked(layer, layers):
    low = flag(layer < layers // 2)
    far, near = low * (layers - 1), (1 - low) * (layers - 1)
    keys = []
    for j in range(layers):
        key = -2 * layers * jnp.abs(layer - j) - j
        key = key - 1000 * layers * flag(far == j) + 1000 * layers * flag(near == j)
        keys.append(key + 5000 * layers * flag(layer == j))
    order = [0] * layers
    for j in range(layers):
        rank = 0
        for other in range(layers):
            if other != j:
                rank = rank + flag(keys[other] < keys[j])
        order = [order[k] + j * flag(rank == k) for k in range(layers)]
    return order


def kernel(
    sizes,
    targets_hbm,
    rhs_hbm,
    inv_hbm,
    blocks_hbm,
    rhs_anc_hbm,
    inv_anc_hbm,
    low_out,
    anc_out,
    rhs,
    inv,
    blocks0,
    blocks1,
    rhs_anc,
    inv_anc,
    x0,
    x1,
    part,
    part_in,
    rhs_t,
    base,
    packed,
    y_in,
    z_out,
    z_in,
    r_in,
    targets,
    load_sem,
    p_send,
    p_recv,
    x_send,
    x_recv,
    y_recv,
    z_recv,
    r_recv,
    send_sem,
):
    layers, rows, cols = sizes
    layer, row, col = (lax.axis_index(a) for a in ("layer", "row", "col"))
    slots = blocks0.shape[0]
    anc_row, narrow, width = rhs_anc.shape
    share = x1.shape[1]
    pieces = anc_row
    raw = pieces // 2
    chips = rows // 2
    last = layers - 1

    chip, core = row // 2, row % 2
    mate = row + 1 - 2 * core
    goal = (row + rows - 1) % rows
    active = goal < cols
    owner = (1 + col) % rows

    loads = [
        pltpu.make_async_copy(source, target, load_sem.at[n])
        for n, source, target in (
            (0, inv_hbm.at[0], inv.at[0]),
            (1, rhs_hbm.at[0], rhs.at[0]),
            (2, blocks_hbm.at[0], blocks0),
            (0, inv_hbm.at[1], inv.at[1]),
            (1, rhs_hbm.at[1], rhs.at[1]),
            (2, blocks_hbm.at[1], blocks1),
            (3, inv_anc_hbm, inv_anc),
            (0, rhs_anc_hbm, rhs_anc),
            (3, targets_hbm, targets),
        )
    ]
    for n in (0, 1):
        loads[n].start()

    barrier = pltpu.get_barrier_semaphore()

    def greet(device):
        pl.semaphore_signal(barrier, inc=1, device_id=device, device_id_type=MESH)

    for d in range(1, rows):
        greet({"row": (row + d) % rows})
    for d in range(1, cols):
        greet({"col": (col + d) % cols})
    for step in (-1, 1):

        @pl.when(jnp.logical_and(layer + step >= 0, layer + step < layers))
        def _():
            greet({"layer": layer + step})

    for cc in range(cols):

        @pl.when(col != cc)
        def _():
            greet({"row": owner, "col": cc})

    @pl.when(jnp.logical_and(active, col != goal))
    def _():
        for r in range(rows):
            greet({"row": r, "col": goal})

    met = (rows - 1) + (cols - 1) + flag(layer > 0) + flag(layer < last)
    met = met + (cols - 1) + flag(jnp.logical_and(active, col != goal)) * rows

    for n in (8, 2):
        loads[n].start()

    order = ranked(layer, layers)

    def spare(j):
        return (1 - j % 2) * last if layers == 4 else layers

    def at(cc, k, h):
        return (cc * rows + k) * pieces + h

    def sends(n):
        return pltpu.make_async_remote_copy(
            src_ref=packed.at[0:n],
            dst_ref=packed.at[0:n],
            send_sem=send_sem,
            recv_sem=send_sem,
            device_id={"row": mate},
            device_id_type=MESH,
        )

    def listed(level, target):
        index, found = jnp.int32(0), jnp.int32(0)
        for s in range(slots):
            hit = (targets[level, s] == target).astype(jnp.int32)
            index = index + hit * s
            found = found + hit
        return (blocks0, blocks1)[level][index], found.astype(F32)

    def span(j):
        return pl.ds(pl.multiple_of(j * share, share), share)

    def solver(k, source):
        if k < 2:
            return [2 * ((source // 2 + 1 + ch) % chips) + k for ch in range(chips)]
        return [2 * ((source // 2 + k - 2) % chips)]

    def place(k):
        return 0 if k < 2 else 1 + (k - 2) // chips

    def p_copy(k, n):
        return pltpu.make_async_remote_copy(
            src_ref=part.at[k],
            dst_ref=part_in.at[place(k), col],
            send_sem=p_send,
            recv_sem=p_recv.at[place(k), col],
            device_id={"row": solver(k, row)[n], "col": goal},
            device_id_type=MESH,
        )

    def here(k, n):
        return jnp.logical_and(goal == col, row == solver(k, row)[n])

    def part_of(k):
        block, found = listed(0, 1)
        part[k] = (dot_t(x0[span(order[k]), :], block) * found).astype(BF16)

    def part_out(k):
        for n in range(len(solver(k, row))):

            @pl.when(jnp.logical_not(here(k, n)))
            def _():
                p_copy(k, n).start()

            @pl.when(here(k, n))
            def _():
                part_in[place(k), col] = part[k]

    def lower(k):
        if share % 128 == 0:
            first = lax.dot_general(
                rhs[0, :, span(order[k])],
                inv[0],
                (((0,), (1,)), ((), ())),
                preferred_element_type=F32,
            )
            x0[span(order[k]), :] = first.astype(BF16)
        elif k == 0:
            first = jnp.dot(inv[0], rhs[0], preferred_element_type=F32)
            x0[...] = first.T.astype(BF16)

    with scope("ldx0"):
        loads[0].wait()
        loads[1].wait()
    for n in (3, 4):
        loads[n].start()
    with scope("x0"):
        lower(0)
    loads[8].wait()
    loads[2].wait()
    for n in (5, 6):
        loads[n].start()

    @pl.when(active)
    def _():
        part_of(0)

    with scope("barr"):
        pl.semaphore_wait(barrier, met)

    with scope("part"):

        @pl.when(active)
        def _():
            part_out(0)
            for k in range(1, rows):
                lower(k)
                part_of(k)
                part_out(k)

        @pl.when(jnp.logical_not(active))
        def _():
            for k in range(1, rows):
                lower(k)

    loads[3].wait()
    loads[7].start()
    loads[4].wait()
    rhs_t[...] = rhs[1].astype(F32).T

    with scope("base"):
        for a in range(anc_row):
            block, found = listed(0, a + 2)
            base[:, a * width : (a + 1) * width] = dot_t(x0[...], block) * found

    for j in range(rows):

        @pl.when(row == j)
        def _():
            low_out[0] = x0[j * share : (j + 1) * share, :].astype(F32).T.astype(BF16)

    def blank(edge, slot, h):
        @pl.when(layer == edge)
        def _():
            z_in[slot, h] = jnp.zeros_like(z_in[slot, h])

    for h in range(pieces):
        if h < raw:
            blank(0, 0, h)
        elif layers == 4:
            blank(0, spare(0), h)
        if h <= raw:
            blank(last, spare(last), h)
        elif layers == 4:
            blank(last, last, h)

    loads[5].wait()

    def mate_copy(k):
        return pltpu.make_async_remote_copy(
            src_ref=x1.at[order[k]],
            dst_ref=x1.at[order[k]],
            send_sem=x_send.at[0],
            recv_sem=x_recv.at[k],
            device_id={"row": mate},
            device_id_type=MESH,
        )

    def x_copy(k, d):
        return pltpu.make_async_remote_copy(
            src_ref=x1.at[order[k]],
            dst_ref=x1.at[order[k]],
            send_sem=x_send.at[place(k)],
            recv_sem=x_recv.at[k],
            device_id={"row": (row + d) % rows},
            device_id_type=MESH,
        )

    def p_sent(n):
        pltpu.make_async_remote_copy(
            src_ref=packed.at[0 : n * cols],
            dst_ref=packed.at[0 : n * cols],
            send_sem=p_send,
            recv_sem=p_send,
            device_id={"row": mate},
            device_id_type=MESH,
        ).wait_send()

    def x_sent(k):
        pltpu.make_async_remote_copy(
            src_ref=x1.at[0 : rows - 1],
            dst_ref=x1.at[0 : rows - 1],
            send_sem=x_send.at[place(k)],
            recv_sem=x_send.at[place(k)],
            device_id={"row": mate},
            device_id_type=MESH,
        ).wait_send()

    def solve(k):
        for cc in range(cols):

            @pl.when(jnp.logical_or(col != cc, row != owner))
            def _():
                pltpu.make_async_remote_copy(
                    src_ref=part.at[0],
                    dst_ref=part_in.at[place(k), cc],
                    send_sem=p_send,
                    recv_sem=p_recv.at[place(k), cc],
                    device_id={"row": mate},
                    device_id_type=MESH,
                ).wait_recv()

        total = part_in[place(k), 0].astype(F32)
        for cc in range(1, cols):
            total = total + part_in[place(k), cc].astype(F32)
        residual = (rhs_t[span(order[k]), :] - total).astype(BF16)
        x1[order[k]] = dot_t(residual, inv[1]).astype(BF16)

    def solve_all(k):
        @pl.when(row == solver(k, owner)[0])
        def _():
            solve(k)
            for d in range(1, rows):
                x_copy(k, d).start()

    def y_copy(d, k, h):
        cc = (col + d) % cols
        return pltpu.make_async_remote_copy(
            src_ref=packed.at[at(cc, k, h)],
            dst_ref=y_in.at[d - 1, k, h],
            send_sem=send_sem,
            recv_sem=y_recv.at[d - 1, k * pieces + h - raw],
            device_id={"col": cc},
            device_id_type=MESH,
        )

    others, whole = range(1, cols), range(1, cols + 1)
    plain = [(h, h + 1) for h in range(0, pieces, 2)]
    mixed = [(h, h + raw) for h in range(pieces - raw)] + [(h,) for h in range(pieces - raw, raw)]

    def products(k):
        @pl.when(core != k if k < 2 else row != solver(k, owner)[0])
        def _():
            mate_copy(k).wait_recv()

        j = order[k]
        for pair in plain if k else mixed:
            for a in pair:
                block, found = listed(1, a + 2)
                lanes = slice(a * width, (a + 1) * width)
                value = base[span(j), lanes] + dot_t(x1[j], block) * found
                value = value.astype(BF16)
                for cc in range(cols):
                    packed[at(cc, k, a)] = value[cc * narrow : (cc + 1) * narrow]
            for a in pair:
                sent(k, a)

    end = jnp.logical_or(layer == 0, layer == last)
    middle = jnp.logical_or(layer == layers // 2 - 1, layer == layers // 2)
    upper = layer == layers // 2
    beside = jnp.logical_or(layer == layers // 2 - 2, layer == layers // 2 + 1)
    low = layer < layers // 2
    high = jnp.logical_not(low)
    onward = layer + 2 * flag(order[0] > layer) - 1


    def sent(k, h):
        if k == 0 and h < raw:

            @pl.when(end)
            def _():
                for d in others:
                    r_copy(d, h).start()
                if h == raw - 1:
                    for n in range(raw):
                        r_copy(cols, n).start()

            if h == raw - 1:

                @pl.when(jnp.logical_and(end, low))
                def _():
                    r_copy(cols, raw).start()

        elif k == 0 and h == raw:

            @pl.when(jnp.logical_and(end, low))
            def _():
                for d in others:
                    r_copy(d, h).start()

            @pl.when(high)
            def _():
                exchange(k, h)

        elif k == rows - 2:
            if h >= raw:

                @pl.when(jnp.logical_and(middle, low) if h == raw else middle)
                def _():
                    for d in others:
                        e_copy(d, h).start()

            if h == pieces - 1:

                @pl.when(middle)
                def _():
                    for n in range(raw + 1, pieces):
                        e_copy(cols, n).start()

                @pl.when(jnp.logical_and(middle, low))
                def _():
                    e_copy(cols, raw).start()

            @pl.when(jnp.logical_not(middle))
            def _():
                exchange(k, h)

        elif k == rows - 1 and h >= raw:

            @pl.when(jnp.logical_not(jnp.logical_and(end, low) if h == raw else end))
            def _():
                exchange(k, h)

        else:
            exchange(k, h)

    def exchange(k, h):
        for d in range(1, cols):
            y_copy(d, k, h).start()

    def r_place(d, h):
        return (d - 1) * (raw + 1) + h if d < cols else (cols - 1) * (raw + 1)

    def r_copy(d, h):
        cc = (col + d) % cols
        return pltpu.make_async_remote_copy(
            src_ref=packed.at[at(cc, 0, h)],
            dst_ref=r_in.at[flag(middle), d - 1, h],
            send_sem=send_sem,
            recv_sem=r_recv.at[flag(middle), r_place(d, h)],
            device_id={"layer": onward},
            device_id_type=MESH,
        )

    def r_wait(slot, d, h, n):
        where = r_in.at[slot, d - 1, 0:n] if n else r_in.at[slot, d - 1, h]
        pltpu.make_async_remote_copy(
            src_ref=where,
            dst_ref=where,
            send_sem=send_sem,
            recv_sem=r_recv.at[slot, r_place(d, h)],
            device_id={"layer": onward},
            device_id_type=MESH,
        ).wait_recv()

    def r_add(slot, k, d, h, place=0):
        cc = (col + d) % cols
        value = packed[at(cc, k, h)].astype(F32) + r_in[slot, d - 1, h - place].astype(F32)
        packed[at(cc, k, h)] = value.astype(BF16)

    def r_others(slot, k, wider, then):
        for h in range(raw):
            for d in others:
                r_wait(slot, d, h, 0)
                r_add(slot, k, d, h)
            then(h)

        @pl.when(wider)
        def _():
            for d in others:
                r_wait(slot, d, raw, 0)
                r_add(slot, k, d, raw)
            then(raw)

    def r_own(slot, k, wider, then):
        for n, case in ((raw, jnp.logical_not(wider)), (raw + 1, wider)):

            @pl.when(case)
            def _():
                r_wait(slot, cols, 0, n)
                for h in range(n):
                    r_add(slot, k, cols, h)
                    then(h)

    def e_copy(d, h):
        cc = (col + d) % cols
        return pltpu.make_async_remote_copy(
            src_ref=packed.at[at(cc, rows - 2, h)],
            dst_ref=r_in.at[0, d - 1, h - raw],
            send_sem=send_sem,
            recv_sem=r_recv.at[0, r_place(d, h - raw)],
            device_id={"layer": order[rows - 2]},
            device_id_type=MESH,
        )

    def e_own(n):
        where = r_in.at[0, cols - 1, pieces - raw - n : pieces - raw]
        pltpu.make_async_remote_copy(
            src_ref=where,
            dst_ref=where,
            send_sem=send_sem,
            recv_sem=r_recv.at[0, r_place(cols, 0)],
            device_id={"layer": onward},
            device_id_type=MESH,
        ).wait_recv()
        for h in range(pieces - n, pieces):
            r_add(0, rows - 1, cols, h, raw)

    def e_others(h):
        for d in others:
            r_wait(0, d, h - raw, 0)
            r_add(0, rows - 1, d, h, raw)
        exchange(rows - 1, h)

    def z_copy(k, h):
        j = order[k]
        toward = layer + 2 * flag(j > layer) - 1
        if k == 0:
            toward = toward + flag(middle) * (j - toward)
        other = jnp.logical_and(j == toward, j < layer)
        if k == 0:
            other = jnp.logical_and(j == toward, jnp.logical_xor(j < layer, middle))
        slot = j + flag(other) * (spare(j) - j)
        return pltpu.make_async_remote_copy(
            src_ref=z_out.at[k, h],
            dst_ref=z_in.at[slot, h],
            send_sem=send_sem,
            recv_sem=z_recv.at[slot, h],
            device_id={"layer": toward},
            device_id_type=MESH,
        )

    def z_wait(slot, h):
        pltpu.make_async_remote_copy(
            src_ref=z_out.at[0, h],
            dst_ref=z_in.at[slot, h],
            send_sem=send_sem,
            recv_sem=z_recv.at[slot, h],
            device_id={"layer": (layer + 1) % layers},
            device_id_type=MESH,
        ).wait_recv()

    def merged(k, h):
        for d in range(1, cols):
            y_copy(d, k, h).wait_recv()
        value = packed[at(col, k, h)].astype(F32)
        for d in range(1, cols):
            value = value + y_in[d - 1, k, h].astype(F32)
        return value

    def merge(k, h):
        with scope("y%d%d" % (k, h)):
            value = merged(k, h)
        j = order[k]
        passing = jnp.logical_or(
            jnp.logical_and(j > layer, layer > 0), jnp.logical_and(j < layer, layer < last)
        )
        if k == rows - 2:
            passing = jnp.logical_and(passing, jnp.logical_not(middle))
            if h == raw:
                passing = jnp.logical_and(passing, jnp.logical_not(jnp.logical_and(beside, low)))
            elif h > raw:
                passing = jnp.logical_and(passing, jnp.logical_not(beside))

        with scope("z%d%d" % (k, h)):

            @pl.when(passing)
            def _():
                z_wait(j, h)
                z_out[k, h] = (value + z_in[j, h].astype(F32)).astype(BF16)

            @pl.when(jnp.logical_not(passing))
            def _():
                z_out[k, h] = value.astype(BF16)

        z_copy(k, h).start()

    def solve_own(k):
        @pl.when(core == k)
        def _():
            with scope("x1"):
                solve(k)
            mate_copy(k).start()

    def first():
        @pl.when(high)
        def _():
            merge(0, raw)

        for h in range(raw + 1, pieces):
            merge(0, h)

    early = [(k, h) for k in range(1, rows - 2) for h in range(pieces)]
    late = [(rows - 2, h) for h in range(pieces)]

    def step(k):
        with scope("p%d" % k):
            products(k)

    solve_own(0)
    solve_own(1)
    far_chip = chip != owner // 2
    swapped = jnp.logical_and(layer == 0, core == 1)
    swap = jnp.logical_and(swapped, far_chip)
    lag = jnp.logical_and(swapped, jnp.logical_not(far_chip))

    @pl.when(swap)
    def _():
        step(1)

    step(0)
    with scope("x1_2"):
        solve_all(2)

    @pl.when(jnp.logical_not(swap))
    def _():
        step(1)

    with scope("x1_3"):
        for k in range(3, rows):
            solve_all(k)

    @pl.when(jnp.logical_not(end))
    def _():
        with scope("rf1"):
            r_others(0, 0, low, lambda h: [r_copy(d, h).start() for d in others])

    ahead = jnp.logical_or(jnp.logical_and(end, far_chip), lag)

    @pl.when(jnp.logical_and(end, jnp.logical_not(lag)))
    def _():
        first()

    @pl.when(ahead)
    def _():
        for k, h in early[:raw]:
            merge(k, h)

    for k in range(2, rows - 1):
        step(k)

    @pl.when(jnp.logical_and(end, jnp.logical_not(ahead)))
    def _():
        for k, h in early[:raw]:
            merge(k, h)

    @pl.when(jnp.logical_not(end))
    def _():
        with scope("rf2"):
            r_own(0, 0, low, lambda h: r_copy(cols, h).start())

    @pl.when(middle)
    def _():
        with scope("rn"):
            r_others(1, rows - 2, high, lambda h: exchange(rows - 2, h))

    step(rows - 1)
    low_out[1] = x1[row].astype(F32).T.astype(BF16)

    @pl.when(middle)
    def _():
        first()

        for k, h in early[:raw]:
            merge(k, h)

        with scope("rw"):
            r_own(1, rows - 2, high, lambda h: None)

        for k, h in late[:raw]:
            merge(k, h)

        @pl.when(upper)
        def _():
            merge(rows - 2, raw)

        for k, h in early[raw:]:
            merge(k, h)

    @pl.when(jnp.logical_not(middle))
    def _():
        @pl.when(jnp.logical_not(end))
        def _():
            first()

        @pl.when(jnp.logical_not(end))
        def _():
            for k, h in early[:raw]:
                merge(k, h)

        for k, h in early[raw : raw + 1]:
            merge(k, h)

        @pl.when(lag)
        def _():
            first()

        for k, h in early[raw + 1 :] + late[:raw]:
            merge(k, h)

        with scope("e"):

            @pl.when(jnp.logical_and(end, low))
            def _():
                e_others(raw)

            @pl.when(end)
            def _():
                for h in range(raw + 1, pieces):
                    e_others(h)

        for k, h in late[raw:]:
            merge(k, h)

        with scope("ew"):

            @pl.when(jnp.logical_and(end, low))
            def _():
                e_own(pieces - raw)

            @pl.when(jnp.logical_and(end, high))
            def _():
                e_own(pieces - raw - 1)

    loads[6].wait()
    loads[7].wait()
    for h in range(pieces):
        with scope("zown%d" % h):
            below, above = layer >= 0, layer >= 0
            if h < raw:
                below = layer != 0
            elif layers == 4:
                above = layer != 0
            if h <= raw:
                above = jnp.logical_and(above, layer != last)
            elif layers == 4:
                below = jnp.logical_and(below, layer != last)
            for slot, case in ((layer, below), (spare(layer), above)):

                @pl.when(case)
                def _():
                    z_wait(slot, h)

        with scope("yown%d" % h):
            value = merged(rows - 1, h)
        with scope("fin%d" % h):
            value = value + z_in[layer, h].astype(F32) + z_in[spare(layer), h].astype(F32)
            residual = (rhs_anc[h].astype(F32) - value).astype(BF16)
            anc_out[h] = dot_t(residual, inv_anc[h])

    with scope("sent"):
        total = 2 * chips + rows - 2
        mine = goal == col
        for n, case in (
            (total, jnp.logical_not(mine)),
            (total - 2, jnp.logical_and(mine, core == 0)),
            (total - 1, jnp.logical_and(mine, core == 1)),
        ):

            @pl.when(jnp.logical_and(active, case))
            def _():
                p_sent(n)

        mate_copy(0).wait_send()
        for k in range(2, rows):

            @pl.when(row == solver(k, owner)[0])
            def _():
                x_sent(k)

        every = pieces * (cols - 1)
        for side, out, back in ((low, raw + 1, raw), (high, raw, raw + 1)):
            kept = out * cols + (pieces - out) * cols + every * (rows - 2) + pieces * (rows - 3)
            near = back * cols + (pieces - back) * cols

            @pl.when(jnp.logical_and(side, middle))
            def _():
                sends(kept + near).wait_send()

            @pl.when(jnp.logical_and(side, jnp.logical_not(middle)))
            def _():
                sends(kept + every + pieces).wait_send()


def hand_over(low, anc, low_out, anc_out, sem):
    first = pltpu.make_async_copy(anc, anc_out, sem.at[0])
    second = pltpu.make_async_copy(low, low_out, sem.at[1])
    first.start()
    second.start()
    first.wait()
    second.wait()


def on_device(sizes, rhs_low, inv_low, blocks, targets, rhs_anc, inv_anc):
    layers, rows, cols = sizes
    levels, slots = blocks.shape[3], blocks.shape[4]
    width, cases = rhs_low.shape[3], rhs_low.shape[4]
    anc_row, narrow = rhs_anc.shape[0], rhs_anc.shape[2]
    share = cases // rows
    pieces, raw = anc_row, anc_row // 2
    chips = rows // 2
    places = 1 + pl.cdiv(rows - 2, chips)
    slots_z = 4 if layers == 4 else layers + 1
    assert levels == 2 and layers == rows and layers % 2 == 0 and layers > 3 and cols <= rows
    assert cols * narrow == share and anc_row % 2 == 0
    any_space = pl.BlockSpec(memory_space=pltpu.HBM)
    dma = pltpu.SemaphoreType.DMA
    low, anc = pl.pallas_call(
        functools.partial(kernel, sizes),
        out_shape=(
            pltpu.VMEM((levels, width, share), BF16),
            pltpu.VMEM((anc_row, narrow, width), F32),
        ),
        in_specs=[any_space] * 6,
        out_specs=(pl.BlockSpec(memory_space=pltpu.VMEM), pl.BlockSpec(memory_space=pltpu.VMEM)),
        scratch_shapes=[
            pltpu.VMEM((levels, width, cases), BF16),
            pltpu.VMEM((levels, width, width), BF16),
            pltpu.VMEM((slots, width, width), BF16),
            pltpu.VMEM((slots, width, width), BF16),
            pltpu.VMEM((anc_row, narrow, width), BF16),
            pltpu.VMEM((anc_row, width, width), BF16),
            pltpu.VMEM((cases, width), BF16),
            pltpu.VMEM((rows, share, width), BF16),
            pltpu.VMEM((rows, share, width), BF16),
            pltpu.VMEM((places, cols, share, width), BF16),
            pltpu.VMEM((cases, width), F32),
            pltpu.VMEM((cases, anc_row * width), F32),
            pltpu.VMEM((cols * rows * pieces, narrow, width), BF16),
            pltpu.VMEM((cols - 1, rows, pieces, narrow, width), BF16),
            pltpu.VMEM((rows - 1, pieces, narrow, width), BF16),
            pltpu.VMEM((slots_z, pieces, narrow, width), BF16),
            pltpu.VMEM((2, cols, raw + 1, narrow, width), BF16),
            pltpu.SMEM((levels, slots), jnp.int32),
            dma((4,)),
            dma,
            dma((places, cols)),
            dma((places,)),
            dma((rows,)),
            dma((cols - 1, rows * pieces - raw)),
            dma((slots_z, pieces)),
            dma((2, (cols - 1) * (raw + 1) + 1)),
            dma,
        ],
        compiler_params=pltpu.CompilerParams(
            collective_id=0, has_side_effects=True, vmem_limit_bytes=56 * 1024 * 1024
        ),
    )(
        targets.reshape(levels, slots),
        rhs_low.reshape(levels, width, cases),
        inv_low.reshape(levels, width, width),
        blocks.reshape(levels, slots, width, width),
        rhs_anc.transpose(0, 2, 1),
        inv_anc,
    )
    low, anc = pl.pallas_call(
        hand_over,
        out_shape=(
            jax.ShapeDtypeStruct(low.shape, low.dtype),
            jax.ShapeDtypeStruct(anc.shape, anc.dtype),
        ),
        in_specs=[pl.BlockSpec(memory_space=pltpu.VMEM)] * 2,
        out_specs=(any_space, any_space),
        scratch_shapes=[dma((2,))],
        compiler_params=pltpu.CompilerParams(vmem_limit_bytes=4 * 1024 * 1024),
    )(low, anc)
    return low[None, :, None], anc.transpose(0, 2, 1)


def solution(mesh):
    sizes = tuple(mesh.shape[a] for a in ("layer", "row", "col"))
    in_specs = (
        P("layer", None, "col", None, None),
        P("layer", None, "col", None, None),
        P("layer", "row", "col", None, None, None, None),
        P("layer", "row", "col", None, None),
        P("row", None, ("layer", "col")),
        P("row", None, None),
    )
    out_specs = (P("layer", None, "col", None, "row"), P("row", None, ("layer", "col")))
    return jax.shard_map(
        functools.partial(on_device, sizes),
        mesh=mesh,
        in_specs=in_specs,
        out_specs=out_specs,
        check_vma=False,
    )
```

```python
import contextlib
import functools

import jax
import jax.numpy as jnp
from jax import lax
from jax.experimental import pallas as pl
from jax.experimental.pallas import tpu as pltpu
from jax.sharding import PartitionSpec as P

MESH = pl.DeviceIdType.MESH
F32 = jnp.float32
BF16 = jnp.bfloat16


def scope(name):
    return contextlib.nullcontext()


def dot_t(left, right):
    return lax.dot_general(left, right, (((1,), (1,)), ((), ())), preferred_element_type=F32)


def flag(condition):
    return condition.astype(jnp.int32)


def ranked(layer, layers):
    low = flag(layer < layers // 2)
    far, near = low * (layers - 1), (1 - low) * (layers - 1)
    keys = []
    for j in range(layers):
        key = -2 * layers * jnp.abs(layer - j) - j
        key = key - 1000 * layers * flag(far == j) + 1000 * layers * flag(near == j)
        keys.append(key + 5000 * layers * flag(layer == j))
    order = [0] * layers
    for j in range(layers):
        rank = 0
        for other in range(layers):
            if other != j:
                rank = rank + flag(keys[other] < keys[j])
        order = [order[k] + j * flag(rank == k) for k in range(layers)]
    return order


def kernel(
    sizes,
    targets_hbm,
    rhs_hbm,
    inv_hbm,
    blocks_hbm,
    rhs_anc_hbm,
    inv_anc_hbm,
    low_out,
    anc_out,
    rhs,
    inv,
    blocks0,
    blocks1,
    rhs_anc,
    inv_anc,
    x0,
    x1,
    part,
    part_in,
    rhs_t,
    base,
    packed,
    y_in,
    z_out,
    z_in,
    r_in,
    targets,
    load_sem,
    p_send,
    p_recv,
    x_send,
    x_recv,
    y_recv,
    z_recv,
    r_recv,
    send_sem,
):
    layers, rows, cols = sizes
    layer, row, col = (lax.axis_index(a) for a in ("layer", "row", "col"))
    slots = blocks0.shape[0]
    anc_row, narrow, width = rhs_anc.shape
    share = x1.shape[1]
    pieces = anc_row
    raw = pieces // 2
    chips = rows // 2
    last = layers - 1

    chip, core = row // 2, row % 2
    mate = row + 1 - 2 * core
    goal = (row + rows - 1) % rows
    active = goal < cols
    owner = (1 + col) % rows

    loads = [
        pltpu.make_async_copy(source, target, load_sem.at[n])
        for n, source, target in (
            (0, inv_hbm.at[0], inv.at[0]),
            (1, rhs_hbm.at[0], rhs.at[0]),
            (2, blocks_hbm.at[0], blocks0),
            (0, inv_hbm.at[1], inv.at[1]),
            (1, rhs_hbm.at[1], rhs.at[1]),
            (2, blocks_hbm.at[1], blocks1),
            (3, inv_anc_hbm, inv_anc),
            (0, rhs_anc_hbm, rhs_anc),
            (3, targets_hbm, targets),
        )
    ]
    for n in (0, 1):
        loads[n].start()

    barrier = pltpu.get_barrier_semaphore()

    def greet(device):
        pl.semaphore_signal(barrier, inc=1, device_id=device, device_id_type=MESH)

    for d in range(1, rows):
        greet({"row": (row + d) % rows})
    for d in range(1, cols):
        greet({"col": (col + d) % cols})
    for step in (-1, 1):

        @pl.when(jnp.logical_and(layer + step >= 0, layer + step < layers))
        def _():
            greet({"layer": layer + step})

    for cc in range(cols):

        @pl.when(col != cc)
        def _():
            greet({"row": owner, "col": cc})

    @pl.when(jnp.logical_and(active, col != goal))
    def _():
        for r in range(rows):
            greet({"row": r, "col": goal})

    met = (rows - 1) + (cols - 1) + flag(layer > 0) + flag(layer < last)
    met = met + (cols - 1) + flag(jnp.logical_and(active, col != goal)) * rows

    for n in (8, 2):
        loads[n].start()

    order = ranked(layer, layers)

    def spare(j):
        return (1 - j % 2) * last if layers == 4 else layers

    def at(cc, k, h):
        return (cc * rows + k) * pieces + h

    def sends(n):
        return pltpu.make_async_remote_copy(
            src_ref=packed.at[0:n],
            dst_ref=packed.at[0:n],
            send_sem=send_sem,
            recv_sem=send_sem,
            device_id={"row": mate},
            device_id_type=MESH,
        )

    def listed(level, target):
        index, found = jnp.int32(0), jnp.int32(0)
        for s in range(slots):
            hit = (targets[level, s] == target).astype(jnp.int32)
            index = index + hit * s
            found = found + hit
        return (blocks0, blocks1)[level][index], found.astype(F32)

    def span(j):
        return pl.ds(pl.multiple_of(j * share, share), share)

    def solver(k, source):
        if k < 2:
            return [2 * ((source // 2 + 1 + ch) % chips) + k for ch in range(chips)]
        return [2 * ((source // 2 + k - 2) % chips)]

    def place(k):
        return 0 if k < 2 else 1 + (k - 2) // chips

    def p_copy(k, n):
        return pltpu.make_async_remote_copy(
            src_ref=part.at[k],
            dst_ref=part_in.at[place(k), col],
            send_sem=p_send,
            recv_sem=p_recv.at[place(k), col],
            device_id={"row": solver(k, row)[n], "col": goal},
            device_id_type=MESH,
        )

    def here(k, n):
        return jnp.logical_and(goal == col, row == solver(k, row)[n])

    def part_of(k):
        block, found = listed(0, 1)
        part[k] = (dot_t(x0[span(order[k]), :], block) * found).astype(BF16)

    def part_out(k):
        for n in range(len(solver(k, row))):

            @pl.when(jnp.logical_not(here(k, n)))
            def _():
                p_copy(k, n).start()

            @pl.when(here(k, n))
            def _():
                part_in[place(k), col] = part[k]

    def lower(k):
        if share % 128 == 0:
            first = lax.dot_general(
                rhs[0, :, span(order[k])],
                inv[0],
                (((0,), (1,)), ((), ())),
                preferred_element_type=F32,
            )
            x0[span(order[k]), :] = first.astype(BF16)
        elif k == 0:
            first = jnp.dot(inv[0], rhs[0], preferred_element_type=F32)
            x0[...] = first.T.astype(BF16)

    with scope("ldx0"):
        loads[0].wait()
        loads[1].wait()
    for n in (3, 4):
        loads[n].start()
    with scope("x0"):
        lower(0)
    loads[8].wait()
    loads[2].wait()
    for n in (5, 6):
        loads[n].start()

    @pl.when(active)
    def _():
        part_of(0)

    with scope("barr"):
        pl.semaphore_wait(barrier, met)

    with scope("part"):

        @pl.when(active)
        def _():
            part_out(0)
            for k in range(1, rows):
                lower(k)
                part_of(k)
                part_out(k)

        @pl.when(jnp.logical_not(active))
        def _():
            for k in range(1, rows):
                lower(k)

    loads[3].wait()
    loads[7].start()
    loads[4].wait()
    rhs_t[...] = rhs[1].astype(F32).T

    with scope("base"):
        for a in range(anc_row):
            block, found = listed(0, a + 2)
            base[:, a * width : (a + 1) * width] = dot_t(x0[...], block) * found

    for j in range(rows):

        @pl.when(row == j)
        def _():
            low_out[0] = x0[j * share : (j + 1) * share, :].astype(F32).T.astype(BF16)

    def blank(edge, slot, h):
        @pl.when(layer == edge)
        def _():
            z_in[slot, h] = jnp.zeros_like(z_in[slot, h])

    for h in range(pieces):
        if h < raw:
            blank(0, 0, h)
        elif layers == 4:
            blank(0, spare(0), h)
        if h <= raw:
            blank(last, spare(last), h)
        elif layers == 4:
            blank(last, last, h)

    loads[5].wait()

    def mate_copy(k):
        return pltpu.make_async_remote_copy(
            src_ref=x1.at[order[k]],
            dst_ref=x1.at[order[k]],
            send_sem=x_send.at[0],
            recv_sem=x_recv.at[k],
            device_id={"row": mate},
            device_id_type=MESH,
        )

    def x_copy(k, d):
        return pltpu.make_async_remote_copy(
            src_ref=x1.at[order[k]],
            dst_ref=x1.at[order[k]],
            send_sem=x_send.at[place(k)],
            recv_sem=x_recv.at[k],
            device_id={"row": (row + d) % rows},
            device_id_type=MESH,
        )

    def p_sent(n):
        pltpu.make_async_remote_copy(
            src_ref=packed.at[0 : n * cols],
            dst_ref=packed.at[0 : n * cols],
            send_sem=p_send,
            recv_sem=p_send,
            device_id={"row": mate},
            device_id_type=MESH,
        ).wait_send()

    def x_sent(k):
        pltpu.make_async_remote_copy(
            src_ref=x1.at[0 : rows - 1],
            dst_ref=x1.at[0 : rows - 1],
            send_sem=x_send.at[place(k)],
            recv_sem=x_send.at[place(k)],
            device_id={"row": mate},
            device_id_type=MESH,
        ).wait_send()

    def solve(k):
        for cc in range(cols):

            @pl.when(jnp.logical_or(col != cc, row != owner))
            def _():
                pltpu.make_async_remote_copy(
                    src_ref=part.at[0],
                    dst_ref=part_in.at[place(k), cc],
                    send_sem=p_send,
                    recv_sem=p_recv.at[place(k), cc],
                    device_id={"row": mate},
                    device_id_type=MESH,
                ).wait_recv()

        total = part_in[place(k), 0].astype(F32)
        for cc in range(1, cols):
            total = total + part_in[place(k), cc].astype(F32)
        residual = (rhs_t[span(order[k]), :] - total).astype(BF16)
        x1[order[k]] = dot_t(residual, inv[1]).astype(BF16)

    def solve_all(k):
        @pl.when(row == solver(k, owner)[0])
        def _():
            solve(k)
            for d in range(1, rows):
                x_copy(k, d).start()

    def y_copy(d, k, h):
        cc = (col + d) % cols
        return pltpu.make_async_remote_copy(
            src_ref=packed.at[at(cc, k, h)],
            dst_ref=y_in.at[d - 1, k, h],
            send_sem=send_sem,
            recv_sem=y_recv.at[d - 1, k * pieces + h - raw],
            device_id={"col": cc},
            device_id_type=MESH,
        )

    others, whole = range(1, cols), range(1, cols + 1)
    plain = [(h, h + 1) for h in range(0, pieces, 2)]
    mixed = [(h, h + raw) for h in range(pieces - raw)] + [(h,) for h in range(pieces - raw, raw)]

    def products(k):
        @pl.when(core != k if k < 2 else row != solver(k, owner)[0])
        def _():
            mate_copy(k).wait_recv()

        j = order[k]
        for pair in plain if k else mixed:
            for a in pair:
                block, found = listed(1, a + 2)
                lanes = slice(a * width, (a + 1) * width)
                value = base[span(j), lanes] + dot_t(x1[j], block) * found
                value = value.astype(BF16)
                for cc in range(cols):
                    packed[at(cc, k, a)] = value[cc * narrow : (cc + 1) * narrow]
            for a in pair:
                sent(k, a)

    end = jnp.logical_or(layer == 0, layer == last)
    middle = jnp.logical_or(layer == layers // 2 - 1, layer == layers // 2)
    upper = layer == layers // 2
    beside = jnp.logical_or(layer == layers // 2 - 2, layer == layers // 2 + 1)
    low = layer < layers // 2
    high = jnp.logical_not(low)
    onward = layer + 2 * flag(order[0] > layer) - 1


    def sent(k, h):
        if k == 0 and h < raw:

            @pl.when(end)
            def _():
                for d in others:
                    r_copy(d, h).start()
                if h == raw - 1:
                    for n in range(raw):
                        r_copy(cols, n).start()

            if h == raw - 1:

                @pl.when(jnp.logical_and(end, low))
                def _():
                    r_copy(cols, raw).start()

        elif k == 0 and h == raw:

            @pl.when(jnp.logical_and(end, low))
            def _():
                for d in others:
                    r_copy(d, h).start()

            @pl.when(high)
            def _():
                exchange(k, h)

        elif k == rows - 2:
            if h >= raw:

                @pl.when(jnp.logical_and(middle, low) if h == raw else middle)
                def _():
                    for d in others:
                        e_copy(d, h).start()

            if h == pieces - 1:

                @pl.when(middle)
                def _():
                    for n in range(raw + 1, pieces):
                        e_copy(cols, n).start()

                @pl.when(jnp.logical_and(middle, low))
                def _():
                    e_copy(cols, raw).start()

            @pl.when(jnp.logical_not(middle))
            def _():
                exchange(k, h)

        elif k == rows - 1 and h >= raw:

            @pl.when(jnp.logical_not(jnp.logical_and(end, low) if h == raw else end))
            def _():
                exchange(k, h)

        else:
            exchange(k, h)

    def exchange(k, h):
        for d in range(1, cols):
            y_copy(d, k, h).start()

    def r_place(d, h):
        return (d - 1) * (raw + 1) + h if d < cols else (cols - 1) * (raw + 1)

    def r_copy(d, h):
        cc = (col + d) % cols
        return pltpu.make_async_remote_copy(
            src_ref=packed.at[at(cc, 0, h)],
            dst_ref=r_in.at[flag(middle), d - 1, h],
            send_sem=send_sem,
            recv_sem=r_recv.at[flag(middle), r_place(d, h)],
            device_id={"layer": onward},
            device_id_type=MESH,
        )

    def r_wait(slot, d, h, n):
        where = r_in.at[slot, d - 1, 0:n] if n else r_in.at[slot, d - 1, h]
        pltpu.make_async_remote_copy(
            src_ref=where,
            dst_ref=where,
            send_sem=send_sem,
            recv_sem=r_recv.at[slot, r_place(d, h)],
            device_id={"layer": onward},
            device_id_type=MESH,
        ).wait_recv()

    def r_add(slot, k, d, h, place=0):
        cc = (col + d) % cols
        value = packed[at(cc, k, h)].astype(F32) + r_in[slot, d - 1, h - place].astype(F32)
        packed[at(cc, k, h)] = value.astype(BF16)

    def r_others(slot, k, wider, then):
        for h in range(raw):
            for d in others:
                r_wait(slot, d, h, 0)
                r_add(slot, k, d, h)
            then(h)

        @pl.when(wider)
        def _():
            for d in others:
                r_wait(slot, d, raw, 0)
                r_add(slot, k, d, raw)
            then(raw)

    def r_own(slot, k, wider, then):
        for n, case in ((raw, jnp.logical_not(wider)), (raw + 1, wider)):

            @pl.when(case)
            def _():
                r_wait(slot, cols, 0, n)
                for h in range(n):
                    r_add(slot, k, cols, h)
                    then(h)

    def e_copy(d, h):
        cc = (col + d) % cols
        return pltpu.make_async_remote_copy(
            src_ref=packed.at[at(cc, rows - 2, h)],
            dst_ref=r_in.at[0, d - 1, h - raw],
            send_sem=send_sem,
            recv_sem=r_recv.at[0, r_place(d, h - raw)],
            device_id={"layer": order[rows - 2]},
            device_id_type=MESH,
        )

    def e_own(n):
        where = r_in.at[0, cols - 1, pieces - raw - n : pieces - raw]
        pltpu.make_async_remote_copy(
            src_ref=where,
            dst_ref=where,
            send_sem=send_sem,
            recv_sem=r_recv.at[0, r_place(cols, 0)],
            device_id={"layer": onward},
            device_id_type=MESH,
        ).wait_recv()
        for h in range(pieces - n, pieces):
            r_add(0, rows - 1, cols, h, raw)

    def e_others(h):
        for d in others:
            r_wait(0, d, h - raw, 0)
            r_add(0, rows - 1, d, h, raw)
        exchange(rows - 1, h)

    def z_copy(k, h):
        j = order[k]
        toward = layer + 2 * flag(j > layer) - 1
        if k == 0:
            toward = toward + flag(middle) * (j - toward)
        other = jnp.logical_and(j == toward, j < layer)
        if k == 0:
            other = jnp.logical_and(j == toward, jnp.logical_xor(j < layer, middle))
        slot = j + flag(other) * (spare(j) - j)
        return pltpu.make_async_remote_copy(
            src_ref=z_out.at[k, h],
            dst_ref=z_in.at[slot, h],
            send_sem=send_sem,
            recv_sem=z_recv.at[slot, h],
            device_id={"layer": toward},
            device_id_type=MESH,
        )

    def z_wait(slot, h):
        pltpu.make_async_remote_copy(
            src_ref=z_out.at[0, h],
            dst_ref=z_in.at[slot, h],
            send_sem=send_sem,
            recv_sem=z_recv.at[slot, h],
            device_id={"layer": (layer + 1) % layers},
            device_id_type=MESH,
        ).wait_recv()

    def merged(k, h):
        for d in range(1, cols):
            y_copy(d, k, h).wait_recv()
        value = packed[at(col, k, h)].astype(F32)
        for d in range(1, cols):
            value = value + y_in[d - 1, k, h].astype(F32)
        return value

    def merge(k, h):
        with scope("y%d%d" % (k, h)):
            value = merged(k, h)
        j = order[k]
        passing = jnp.logical_or(
            jnp.logical_and(j > layer, layer > 0), jnp.logical_and(j < layer, layer < last)
        )
        if k == rows - 2:
            passing = jnp.logical_and(passing, jnp.logical_not(middle))
            if h == raw:
                passing = jnp.logical_and(passing, jnp.logical_not(jnp.logical_and(beside, low)))
            elif h > raw:
                passing = jnp.logical_and(passing, jnp.logical_not(beside))

        with scope("z%d%d" % (k, h)):

            @pl.when(passing)
            def _():
                z_wait(j, h)
                z_out[k, h] = (value + z_in[j, h].astype(F32)).astype(BF16)

            @pl.when(jnp.logical_not(passing))
            def _():
                z_out[k, h] = value.astype(BF16)

        z_copy(k, h).start()

    def solve_own(k):
        @pl.when(core == k)
        def _():
            with scope("x1"):
                solve(k)
            mate_copy(k).start()

    def first():
        @pl.when(high)
        def _():
            merge(0, raw)

        for h in range(raw + 1, pieces):
            merge(0, h)

    early = [(k, h) for k in range(1, rows - 2) for h in range(pieces)]
    late = [(rows - 2, h) for h in range(pieces)]

    def step(k):
        with scope("p%d" % k):
            products(k)

    solve_own(0)
    solve_own(1)
    step(0)
    with scope("x1_2"):
        solve_all(2)
    step(1)
    with scope("x1_3"):
        for k in range(3, rows):
            solve_all(k)

    @pl.when(jnp.logical_not(end))
    def _():
        with scope("rf1"):
            r_others(0, 0, low, lambda h: [r_copy(d, h).start() for d in others])

    beyond = jnp.logical_and(end, chip != owner // 2)

    @pl.when(end)
    def _():
        first()

    @pl.when(beyond)
    def _():
        for k, h in early[:raw]:
            merge(k, h)

    for k in range(2, rows - 1):
        step(k)

    @pl.when(jnp.logical_and(end, jnp.logical_not(beyond)))
    def _():
        for k, h in early[:raw]:
            merge(k, h)

    @pl.when(jnp.logical_not(end))
    def _():
        with scope("rf2"):
            r_own(0, 0, low, lambda h: r_copy(cols, h).start())

    @pl.when(middle)
    def _():
        with scope("rn"):
            r_others(1, rows - 2, high, lambda h: exchange(rows - 2, h))

    step(rows - 1)
    low_out[1] = x1[row].astype(F32).T.astype(BF16)

    @pl.when(middle)
    def _():
        first()

        for k, h in early[:raw]:
            merge(k, h)

        @pl.when(upper)
        def _():
            for k, h in early[raw : raw + 1]:
                merge(k, h)

        with scope("rw"):
            r_own(1, rows - 2, high, lambda h: None)

        for k, h in late[:raw]:
            merge(k, h)

        @pl.when(upper)
        def _():
            merge(rows - 2, raw)

        @pl.when(jnp.logical_not(upper))
        def _():
            for k, h in early[raw : raw + 1]:
                merge(k, h)

        for k, h in early[raw + 1 :]:
            merge(k, h)

    @pl.when(jnp.logical_not(middle))
    def _():
        @pl.when(jnp.logical_not(end))
        def _():
            first()

        @pl.when(jnp.logical_not(end))
        def _():
            for k, h in early[:raw]:
                merge(k, h)

        for k, h in early[raw:] + late[:raw]:
            merge(k, h)

        with scope("e"):

            @pl.when(jnp.logical_and(end, low))
            def _():
                e_others(raw)

            @pl.when(end)
            def _():
                for h in range(raw + 1, pieces):
                    e_others(h)

        for k, h in late[raw:]:
            merge(k, h)

        with scope("ew"):

            @pl.when(jnp.logical_and(end, low))
            def _():
                e_own(pieces - raw)

            @pl.when(jnp.logical_and(end, high))
            def _():
                e_own(pieces - raw - 1)

    loads[6].wait()
    loads[7].wait()
    for h in range(pieces):
        with scope("zown%d" % h):
            below, above = layer >= 0, layer >= 0
            if h < raw:
                below = layer != 0
            elif layers == 4:
                above = layer != 0
            if h <= raw:
                above = jnp.logical_and(above, layer != last)
            elif layers == 4:
                below = jnp.logical_and(below, layer != last)
            for slot, case in ((layer, below), (spare(layer), above)):

                @pl.when(case)
                def _():
                    z_wait(slot, h)

        with scope("yown%d" % h):
            value = merged(rows - 1, h)
        with scope("fin%d" % h):
            value = value + z_in[layer, h].astype(F32) + z_in[spare(layer), h].astype(F32)
            residual = (rhs_anc[h].astype(F32) - value).astype(BF16)
            anc_out[h] = dot_t(residual, inv_anc[h])

    with scope("sent"):
        total = 2 * chips + rows - 2
        mine = goal == col
        for n, case in (
            (total, jnp.logical_not(mine)),
            (total - 2, jnp.logical_and(mine, core == 0)),
            (total - 1, jnp.logical_and(mine, core == 1)),
        ):

            @pl.when(jnp.logical_and(active, case))
            def _():
                p_sent(n)

        mate_copy(0).wait_send()
        for k in range(2, rows):

            @pl.when(row == solver(k, owner)[0])
            def _():
                x_sent(k)

        every = pieces * (cols - 1)
        for side, out, back in ((low, raw + 1, raw), (high, raw, raw + 1)):
            kept = out * cols + (pieces - out) * cols + every * (rows - 2) + pieces * (rows - 3)
            near = back * cols + (pieces - back) * cols

            @pl.when(jnp.logical_and(side, middle))
            def _():
                sends(kept + near).wait_send()

            @pl.when(jnp.logical_and(side, jnp.logical_not(middle)))
            def _():
                sends(kept + every + pieces).wait_send()


def hand_over(low, anc, low_out, anc_out, sem):
    first = pltpu.make_async_copy(anc, anc_out, sem.at[0])
    second = pltpu.make_async_copy(low, low_out, sem.at[1])
    first.start()
    second.start()
    first.wait()
    second.wait()


def on_device(sizes, rhs_low, inv_low, blocks, targets, rhs_anc, inv_anc):
    layers, rows, cols = sizes
    levels, slots = blocks.shape[3], blocks.shape[4]
    width, cases = rhs_low.shape[3], rhs_low.shape[4]
    anc_row, narrow = rhs_anc.shape[0], rhs_anc.shape[2]
    share = cases // rows
    pieces, raw = anc_row, anc_row // 2
    chips = rows // 2
    places = 1 + pl.cdiv(rows - 2, chips)
    slots_z = 4 if layers == 4 else layers + 1
    assert levels == 2 and layers == rows and layers % 2 == 0 and layers > 3 and cols <= rows
    assert cols * narrow == share and anc_row % 2 == 0
    any_space = pl.BlockSpec(memory_space=pltpu.HBM)
    dma = pltpu.SemaphoreType.DMA
    low, anc = pl.pallas_call(
        functools.partial(kernel, sizes),
        out_shape=(
            pltpu.VMEM((levels, width, share), BF16),
            pltpu.VMEM((anc_row, narrow, width), F32),
        ),
        in_specs=[any_space] * 6,
        out_specs=(pl.BlockSpec(memory_space=pltpu.VMEM), pl.BlockSpec(memory_space=pltpu.VMEM)),
        scratch_shapes=[
            pltpu.VMEM((levels, width, cases), BF16),
            pltpu.VMEM((levels, width, width), BF16),
            pltpu.VMEM((slots, width, width), BF16),
            pltpu.VMEM((slots, width, width), BF16),
            pltpu.VMEM((anc_row, narrow, width), BF16),
            pltpu.VMEM((anc_row, width, width), BF16),
            pltpu.VMEM((cases, width), BF16),
            pltpu.VMEM((rows, share, width), BF16),
            pltpu.VMEM((rows, share, width), BF16),
            pltpu.VMEM((places, cols, share, width), BF16),
            pltpu.VMEM((cases, width), F32),
            pltpu.VMEM((cases, anc_row * width), F32),
            pltpu.VMEM((cols * rows * pieces, narrow, width), BF16),
            pltpu.VMEM((cols - 1, rows, pieces, narrow, width), BF16),
            pltpu.VMEM((rows - 1, pieces, narrow, width), BF16),
            pltpu.VMEM((slots_z, pieces, narrow, width), BF16),
            pltpu.VMEM((2, cols, raw + 1, narrow, width), BF16),
            pltpu.SMEM((levels, slots), jnp.int32),
            dma((4,)),
            dma,
            dma((places, cols)),
            dma((places,)),
            dma((rows,)),
            dma((cols - 1, rows * pieces - raw)),
            dma((slots_z, pieces)),
            dma((2, (cols - 1) * (raw + 1) + 1)),
            dma,
        ],
        compiler_params=pltpu.CompilerParams(
            collective_id=0,
            has_side_effects=True,
            vmem_limit_bytes=56 * 1024 * 1024,
        ),
    )(
        targets.reshape(levels, slots),
        rhs_low.reshape(levels, width, cases),
        inv_low.reshape(levels, width, width),
        blocks.reshape(levels, slots, width, width),
        rhs_anc.transpose(0, 2, 1),
        inv_anc,
    )
    low, anc = pl.pallas_call(
        hand_over,
        out_shape=(
            jax.ShapeDtypeStruct(low.shape, low.dtype),
            jax.ShapeDtypeStruct(anc.shape, anc.dtype),
        ),
        in_specs=[pl.BlockSpec(memory_space=pltpu.VMEM)] * 2,
        out_specs=(any_space, any_space),
        scratch_shapes=[dma((2,))],
        compiler_params=pltpu.CompilerParams(vmem_limit_bytes=4 * 1024 * 1024),
    )(low, anc)
    return low[None, :, None], anc.transpose(0, 2, 1)


def solution(mesh):
    sizes = tuple(mesh.shape[a] for a in ("layer", "row", "col"))
    in_specs = (
        P("layer", None, "col", None, None),
        P("layer", None, "col", None, None),
        P("layer", "row", "col", None, None, None, None),
        P("layer", "row", "col", None, None),
        P("row", None, ("layer", "col")),
        P("row", None, None),
    )
    out_specs = (P("layer", None, "col", None, "row"), P("row", None, ("layer", "col")))
    return jax.shard_map(
        functools.partial(on_device, sizes),
        mesh=mesh,
        in_specs=in_specs,
        out_specs=out_specs,
        check_vma=False,
    )
```
